32 devices in a mesh: slab: 8 (over z, x), tile: 4 (over y, core).
Axes of the slice: x: 2, y: 2, z: 4, core: 2. Of those that a mesh axis runs over, the one named last changes fastest.
Arguments:
- splat_centers_pixel: float32 [8, 2, 2, 1024], P('slab', None, None, 'tile'), may hold values from 0 to 32
- splat_scale: float32 [8, 2, 2, 1024], P('slab', None, None, 'tile'), may hold values from 1 to 6
- splat_angle: float32 [8, 2, 1024], P('slab', None, 'tile'), may hold values from -3.140625 to 3.140625
- splat_opacity: float32 [8, 1024], P('slab', 'tile'), may hold values from 0.002 to 0.08
- splat_color: float32 [8, 3, 1024], P('slab', None, 'tile'), may hold values from 0 to 1
- depth_rank: int32 [8, 2, 1024], P('slab', None, 'tile'), may hold values from 0 to 1023, each once within a row
- dest_tile: int32 [8, 2, 1024, 1], P('slab', None, 'tile'), may hold values from 0 to 3; in each aligned block of 256 rows (0 to 255, 256 to 511, ..., all dimensions but the last counted through in order) at most 128 rows name the same one
- slab_order: int32 [2, 8], replicated, may hold values from 0 to 7, each once within a row
Outputs:
- image: float32 [4, 4, 4096], P(None, 'tile', 'slab')
The draws below stay inside these ranges and needn't reach their ends.
Inputs may be any that keep to these rules, and one draw needn't show every extreme that they name: `dest_tile`: within each aligned block of 256 rows of a slab and view (the rows of one device), no region is named by more than 128 rows; some region is named by exactly 128 rows in some blocks. `depth_rank`: for each slab and view, every number of 0 to 1023 appears once. `slab_order`: for each view, every slab number appears once.
All inputs are finite; a program needn't handle non-finite values.
Results may differ from the reference program's by a relative error of at most 0.0003.
Values sent between devices are 32-bit elements; how exact they have to be, the bound alone decides.
No kernel may reach another device: no remote copies, remote signals or barrier semaphores. Data moves between devices by JAX's collectives and lax.ppermute only.
A program may use at most 64 MiB of HBM per device.

```python
import math
from functools import partial
import jax
import jax.numpy as jnp
import numpy as np
from jax import lax

VIEWS = 2
PW = 64
PH = 32
ROWS = 256
NROWS = 1024
CAP = 128
N_SLAB = 8
N_TILE = 4


def steps_of(rng, shape, pieces, least, high):
    def one(position, parts):
        draws = jax.random.uniform(jax.random.fold_in(jax.random.fold_in(rng, 6), position), (parts,), jnp.float32, least / len(pieces), high / len(pieces))
        return jnp.repeat(jnp.exp(draws), shape[position] // parts).reshape((-1,) + (1,) * (len(shape) - position - 1))

    loudness = one(*pieces[0])
    for cut in pieces[1:]:
        loudness = loudness * one(*cut)
    return loudness


def deal_out(stream_key, own, number, rows, number_of, top, limit, lean):
    sequence = jax.random.permutation(stream_key, number_of)
    crowded, common = load_shares(number_of, rows * top, limit, lean, True), load_shares(number_of, rows * top, limit, lean, False)
    places = jnp.arange(number_of)

    def named(tallies, turn):
        used = int((tallies > 0).sum())
        fixed = max(1, used // 4)
        shifted = fixed + (places - fixed + turn * (used - fixed)) % max(1, number_of - fixed)
        return jnp.zeros((number_of,), jnp.int32).at[sequence[jnp.where(places < fixed, places, shifted)]].set(jnp.asarray(tallies, jnp.int32))

    tallies = jnp.where(number % 4 == 0, named(crowded, number // 4), named(common, number - number // 4 - 1))
    mixed = jax.random.permutation(jax.random.fold_in(own, 3), number_of)
    giver, sink = mixed[0:number_of // 2 * 2:2], mixed[1:number_of // 2 * 2:2]
    slack = jnp.minimum(tallies[giver] - 1, limit - tallies[sink]) // 2
    slack = jnp.where((giver == sequence[0]) | (sink == sequence[0]) | (tallies[sink] == 0), 0, jnp.maximum(slack, 0))
    shifted = jax.random.randint(jax.random.fold_in(own, 4), (number_of // 2,), 0, 1 << 20) % (slack + 1)
    tallies = tallies.at[giver].add(-shifted).at[sink].add(shifted)
    members = jnp.searchsorted(jnp.cumsum(tallies), jnp.arange(rows * top), side="right").astype(jnp.int32)
    grid = members.reshape(top, rows).T
    grid = grid[jax.random.permutation(jax.random.fold_in(own, 1), rows)]
    turn = jax.random.randint(jax.random.fold_in(own, 2), (rows, 1), 0, top)
    return jnp.take_along_axis(grid, (jnp.arange(top)[None, :] + turn) % top, axis=1)


def load_shares(number_of, total, reach, slope, full):
    loads = [(1 << 20) // math.isqrt(standing ** slope) + 1 for standing in range(1, number_of + 1)]
    largest = reach if full else min(reach, max(-(-total // number_of), total * loads[0] // sum(loads)))
    least = 1 if total - largest >= number_of - 1 else 0
    holding, spare = [largest] + [least] * (number_of - 1), total - largest - least * (number_of - 1)
    while spare > 0:
        free = [i for i in range(1, number_of) if holding[i] < largest] or [i for i in range(1, number_of) if holding[i] < reach]
        whole, budget = sum([loads[i] for i in free]), spare
        for i in free:
            extra = min(reach - holding[i], max(1, budget * loads[i] // whole), spare)
            holding[i] = holding[i] + extra
            spare = spare - extra
    return np.array(holding)


def setup_inputs(seed: int = 0) -> dict:
    key_list = jax.random.split(jax.random.key(seed), 9)
    splat_centers_pixel = jnp.clip(32.0 * jax.random.uniform(key_list[0], (N_SLAB, VIEWS, 2, NROWS), jnp.float32) ** steps_of(key_list[0], (N_SLAB, VIEWS, 2, NROWS), ((0, 8), (3, 4)), -0.2, 0.2), 0.0, 32.0)
    splat_scale = jnp.clip(jnp.exp(math.log(6.0) - 1.7917595 * jax.random.uniform(key_list[1], (N_SLAB, VIEWS, 2, NROWS), jnp.float32) ** steps_of(key_list[1], (N_SLAB, VIEWS, 2, NROWS), ((0, 8), (3, 4)), -0.2, 0.2)), 1.0, 6.0)
    splat_angle = jnp.clip(jax.random.uniform(key_list[2], (N_SLAB, VIEWS, NROWS), jnp.float32, -3.140625, 3.140625), -3.140625, 3.140625)
    splat_opacity = jnp.clip(jnp.exp(math.log(0.08) - 3.6888794 * jax.random.uniform(key_list[3], (N_SLAB, NROWS), jnp.float32) ** steps_of(key_list[3], (N_SLAB, NROWS), ((0, 8), (1, 4)), -0.2, 0.2)), 0.002, 0.08)
    splat_color = jnp.clip(1.0 * jax.random.uniform(key_list[4], (N_SLAB, 3, NROWS), jnp.float32) ** steps_of(key_list[4], (N_SLAB, 3, NROWS), ((0, 8), (2, 4)), -0.2, 0.2), 0.0, 1.0)
    depth_rank = jax.vmap(lambda own: jax.random.permutation(own, NROWS))(jax.random.split(key_list[5], N_SLAB * VIEWS)).reshape((N_SLAB, VIEWS, NROWS)).astype(jnp.int32)
    dest_tile_keys = jax.random.split(jax.random.fold_in(key_list[6], 1), N_SLAB * VIEWS * NROWS // ROWS)
    dest_tile_turns = jax.random.permutation(jax.random.fold_in(key_list[6], 3), N_SLAB * VIEWS * NROWS // ROWS)
    dest_tile = jax.vmap(lambda own, number: deal_out(jax.random.fold_in(key_list[6], 2), own, number, ROWS, N_TILE, 1, CAP, 2))(dest_tile_keys, dest_tile_turns).reshape((N_SLAB, VIEWS, NROWS, 1))
    slab_order = jax.vmap(lambda own: jax.random.permutation(own, N_SLAB))(jax.random.split(key_list[7], VIEWS)).reshape((VIEWS, N_SLAB)).astype(jnp.int32)
    return {"splat_centers_pixel": splat_centers_pixel, "splat_scale": splat_scale, "splat_angle": splat_angle, "splat_opacity": splat_opacity, "splat_color": splat_color, "depth_rank": depth_rank, "dest_tile": dest_tile, "slab_order": slab_order}


def splat_features(centers, splat_extents, angles, opacity_row, color_rows, ranks):
    cosine = jnp.cos(angles)
    sine = jnp.sin(angles)
    inv_major = 1.0 / (splat_extents[:, 0] * splat_extents[:, 0])
    inverse_minor_axis = 1.0 / (splat_extents[:, 1] * splat_extents[:, 1])
    conic_a = cosine * cosine * inv_major + sine * sine * inverse_minor_axis
    conic_b = cosine * sine * (inv_major - inverse_minor_axis)
    conic_c = sine * sine * inv_major + cosine * cosine * inverse_minor_axis
    view_count = centers.shape[0]
    opacity_all = jnp.broadcast_to(opacity_row[None], angles.shape)
    color_all = jnp.broadcast_to(color_rows[None], (view_count,) + color_rows.shape)
    return jnp.concatenate([centers, conic_a[:, None], conic_b[:, None], conic_c[:, None],
                            opacity_all[:, None], color_all, ranks.astype(jnp.float32)[:, None]], axis=1)


def bucket(features, targets, tile_count, capacity):
    onehot_selector = (targets[:, None] == jnp.arange(tile_count, dtype=jnp.int32)[None, :]).astype(jnp.int32)
    preceding_slabs = jnp.cumsum(onehot_selector, axis=0) - onehot_selector
    slots = (targets * capacity + jnp.sum(preceding_slabs * onehot_selector, axis=1)).astype(jnp.int32)
    outgoing = jnp.zeros((features.shape[0], tile_count * capacity), jnp.float32)
    return outgoing.at[:, slots].set(features)


def blend(incoming, width, height):
    pixel = jnp.arange(width * height, dtype=jnp.int32)
    pixel_x = (pixel % width).astype(jnp.float32) + 0.5
    pixel_y = (pixel // width).astype(jnp.float32) + 0.5
    offset_x = pixel_x[:, None] - incoming[0][None, :]
    offset_y = pixel_y[:, None] - incoming[1][None, :]
    quad = incoming[2][None, :] * offset_x * offset_x + 2.0 * incoming[3][None, :] * offset_x * offset_y + incoming[4][None, :] * offset_y * offset_y
    opacity_map = incoming[5][None, :] * jnp.exp(-0.5 * quad)
    log_keep = jnp.log1p(-opacity_map)
    depth_rank = incoming[9]
    precede = (depth_rank[:, None] < depth_rank[None, :]).astype(jnp.float32)
    slab_depth_total = jnp.dot(log_keep, precede, precision=lax.Precision.HIGHEST, preferred_element_type=jnp.float32)
    weights = opacity_map * jnp.exp(slab_depth_total)
    shaded = jnp.dot(weights, incoming[6:9].T, precision=lax.Precision.HIGHEST, preferred_element_type=jnp.float32)
    layer_log_transmit = jnp.sum(log_keep, axis=1)
    return jnp.concatenate([shaded.T, layer_log_transmit[None, :]], axis=0)


def reference(splat_centers_pixel, splat_scale, splat_angle, splat_opacity, splat_color, depth_rank, dest_tile, slab_order):
    capacity = 2 * ROWS // N_TILE
    slots_all = N_TILE * capacity
    pixels = PW * PH

    def one_slab(inputs):
        centers, splat_extents, angles, opacity_row, color_rows, ranks, targets = inputs
        features = splat_features(centers, splat_extents, angles, opacity_row, color_rows, ranks)
        features = features.reshape(VIEWS, 10, N_TILE, ROWS).transpose(0, 2, 1, 3)
        targets = targets[:, :, 0].reshape(VIEWS, N_TILE, ROWS)
        sender = partial(bucket, tile_count=N_TILE, capacity=capacity)
        outgoing = jax.vmap(jax.vmap(sender))(features, targets)
        incoming = outgoing.reshape(VIEWS, N_TILE, 10, N_TILE, capacity).transpose(0, 3, 2, 1, 4)
        incoming = incoming.reshape(VIEWS * N_TILE, 10, slots_all)
        layers = lax.map(lambda lists: blend(lists, PW, PH), incoming)
        return layers.reshape(VIEWS, N_TILE, 4, pixels)

    layers = lax.map(one_slab, (splat_centers_pixel, splat_scale, splat_angle, splat_opacity, splat_color, depth_rank, dest_tile))
    layer_log_transmit = layers[:, :, :, 3]
    layer_color = layers[:, :, :, :3]
    preceding_slabs = (slab_order[:, :, None] < slab_order[:, None, :]).astype(jnp.float32)
    slab_depth_total = jnp.einsum('mcz,cmey->zmey', preceding_slabs, layer_log_transmit, precision=lax.Precision.HIGHEST)
    slab_prefix = jnp.exp(slab_depth_total)
    shaded = jnp.sum(slab_prefix[:, :, :, None, :] * layer_color, axis=0)
    transmit = jnp.exp(jnp.sum(layer_log_transmit, axis=0))
    image = jnp.concatenate([shaded, transmit[:, :, None, :]], axis=2)
    return image.transpose(2, 1, 0, 3).reshape(4, N_TILE, VIEWS * pixels)
```

```python
from functools import partial
import math

import jax
import jax.numpy as jnp
from jax import lax
from jax.experimental import pallas as pl
from jax.experimental.pallas import tpu as pltpu
from jax.sharding import PartitionSpec as P

PW = 64
PH = 32
NF = 10
HALF_LOG2E = 0.5 * math.log2(math.e)
X_MID = 16.0
LANES = 128
COLOR_AT = 32

f32 = jnp.float32
bf16 = jnp.bfloat16
NT = (((1,), (1,)), ((), ()))


def pieces(x, count):
    out = []
    for _ in range(count):
        part = x.astype(bf16)
        out.append(part)
        x = x - part.astype(f32)
    return out


def sender_kernel(views, tiles, copies, direct, centers, scale, angle, opacity, color, rank, dest, out, feat):
    rows = centers.shape[3]
    cap = 2 * rows // tiles
    slots = tiles * cap
    hot_rows = -(-tiles // 16) * 16

    theta = angle[0]
    cosine = jnp.cos(theta)
    sine = jnp.sin(theta)
    feat[...] = jnp.zeros_like(feat)
    before = lax.broadcasted_iota(jnp.int32, (rows, rows), 0) < lax.broadcasted_iota(jnp.int32, (rows, rows), 1)
    before = jnp.where(before, 1.0, 0.0).astype(bf16)
    tile_id = lax.broadcasted_iota(jnp.int32, (hot_rows, rows), 0)
    slot_id = lax.broadcasted_iota(jnp.int32, (slots, rows), 0)
    for v in range(views):
        s1 = scale[0, v, 0:1]
        s2 = scale[0, v, 1:2]
        i1 = 1.0 / (s1 * s1)
        i2 = 1.0 / (s2 * s2)
        c = cosine[v : v + 1]
        s = sine[v : v + 1]
        feat[v, 0:1] = centers[0, v, 0:1]
        feat[v, 1:2] = centers[0, v, 1:2]
        feat[v, 2:3] = c * c * i1 + s * s * i2
        feat[v, 3:4] = c * s * (i1 - i2)
        feat[v, 4:5] = s * s * i1 + c * c * i2
        feat[v, 5:6] = opacity[0:1]
        feat[v, 6:9] = color[0]
        feat[v, 9:10] = rank[0, v : v + 1].astype(f32)

        target = dest[v : v + 1]
        hot = jnp.where(tile_id == target, 1.0, 0.0)
        earlier = jnp.dot(hot.astype(bf16), before, preferred_element_type=f32)
        place = jnp.sum(hot * earlier, axis=0, keepdims=True).astype(jnp.int32)
        slot = target * cap + place
        pick = jnp.where(slot_id == slot, 1.0, 0.0).astype(bf16)
        stack = jnp.concatenate(pieces(feat[v], 3), axis=0)
        moved = lax.dot_general(stack, pick, NT, preferred_element_type=f32)
        moved = moved[0:16] + moved[16:32] + moved[32:48]
        if direct:
            for t in range(tiles):
                for f in range(NF):
                    row = moved[f : f + 1, t * cap : (t + 1) * cap]
                    for q in range(copies):
                        out[(v * copies + q) * tiles + t, :, f * cap : (f + 1) * cap] = row
        else:
            out[v] = moved[0:NF]


def receiver_kernel(slabs, tiles, views, direct, order, recv, out, feat, coef, sorted_rows, sorted_color, basis):
    entries = feat.shape[2]
    cap = entries // tiles
    columns = out.shape[2]
    blocks = columns // LANES
    pixels = PW * PH
    groups = slabs // 8

    me = lax.axis_index("slab")
    first = me * columns
    view = first // pixels
    y_first = (first - view * pixels) // PW
    half_rows = columns // PW // 2
    y_mid = (y_first + half_rows).astype(f32)

    if direct:
        for f in range(NF):
            for t in range(tiles):
                for k in range(slabs):
                    feat[f, k : k + 1, t * cap : (t + 1) * cap] = recv[k * tiles + t, :, f * cap : (f + 1) * cap]
    else:
        feat[...] = recv[...]

    x = feat[0] - X_MID
    y = feat[1] - y_mid
    a = feat[2]
    b = feat[3]
    c = feat[4]
    o = feat[5]
    h = -HALF_LOG2E
    real = o > 0.0
    ax_by = a * x + b * y
    bx_cy = b * x + c * y
    constant = h * (x * ax_by + y * bx_cy) + jnp.where(real, jnp.log2(jnp.where(real, o, 1.0)), -300.0)
    quad = [h * a, (2.0 * h) * b, h * c]
    lin = [(-2.0 * h) * ax_by, (-2.0 * h) * bx_cy, constant]
    coef[...] = jnp.zeros_like(coef)
    at = 0
    for one in quad:
        parts = [p.astype(f32) for p in pieces(one, 3)]
        for p in parts + parts:
            coef[:, at] = p
            at += 1
    for one in lin:
        for p in pieces(one, 3):
            coef[:, at] = p.astype(f32)
            at += 1
    for i in range(3):
        hi, lo = pieces(feat[6 + i], 2)
        coef[:, COLOR_AT + i] = hi.astype(f32)
        coef[:, LANES + COLOR_AT + i] = lo.astype(f32)

    lane = lax.broadcasted_iota(jnp.int32, (1, columns), 1)
    row = lane // PW
    u = (lane - row * PW).astype(f32) + (0.5 - X_MID)
    w = (row - half_rows).astype(f32) + 0.5
    basis_rows = []
    for one in (u * u, u * w, w * w):
        hi, lo = pieces(one, 2)
        basis_rows += [hi.astype(f32)] * 3 + [lo.astype(f32)] * 3
    basis_rows += [u] * 3 + [w] * 3 + [jnp.ones_like(u)] * 3
    basis[...] = jnp.zeros_like(basis)
    for i, one in enumerate(basis_rows):
        basis[i : i + 1] = one
    monomials = basis[...].astype(bf16)

    lane_e = lax.broadcasted_iota(jnp.int32, (slabs, entries), 1).astype(f32)
    ranks = jnp.where(real, feat[9], lane_e + 1048576.0)
    ranks_t = ranks.T
    chunk = 128
    for k in range(slabs):
        mine = ranks[k : k + 1]
        count = jnp.zeros((8, entries), f32)
        for i in range(entries // 8):
            other = ranks_t[i * 8 : (i + 1) * 8, k : k + 1]
            count = count + jnp.where(other < mine, 1.0, 0.0)
        position = jnp.sum(count, axis=0, keepdims=True).astype(jnp.int32)
        table = coef[k].astype(bf16)
        for j in range(entries // chunk):
            want = lax.broadcasted_iota(jnp.int32, (chunk, entries), 0) + j * chunk
            pick = jnp.where(want == position, 1.0, 0.0).astype(bf16)
            got = lax.dot_general(pick, table, NT, preferred_element_type=f32)
            low = got[:, 0:LANES]
            sorted_rows[pl.ds(j * chunk * slabs + k, chunk, stride=slabs), :] = low
            sorted_color[pl.ds(j * chunk * slabs + k, chunk, stride=slabs), :] = low + got[:, LANES:]

    steps = 256 // slabs
    def blend(i, carry):
        keep, shade = carry
        keep = list(keep)
        shade = list(shade)
        base = pl.multiple_of(i * 256, 256)
        lhs = sorted_rows[pl.ds(base, 256), :].astype(bf16)
        expo = jnp.dot(lhs, monomials, preferred_element_type=f32)
        colors = sorted_color[pl.ds(base, 256), :]
        for s in range(steps):
            for g in range(groups):
                r = (s * groups + g) * 8
                cols = [
                    jnp.broadcast_to(colors[r : r + 8, COLOR_AT + n : COLOR_AT + n + 1], (8, LANES)) for n in range(3)
                ]
                for l in range(blocks):
                    n = g * blocks + l
                    alpha = jnp.exp2(expo[r : r + 8, l * LANES : (l + 1) * LANES])
                    weight = alpha * keep[n]
                    keep[n] = keep[n] - weight
                    for m in range(3):
                        shade[n * 3 + m] = shade[n * 3 + m] + weight * cols[m]
        return tuple(keep), tuple(shade)

    ones = jnp.ones((8, LANES), f32)
    zeros = jnp.zeros((8, LANES), f32)
    state = ((ones,) * (groups * blocks), (zeros,) * (groups * blocks * 3))
    keep, shade = lax.fori_loop(0, entries * slabs // 256, blend, state)

    sub = lax.broadcasted_iota(jnp.int32, (8, LANES), 0)
    orders = []
    for g in range(groups):
        mine = jnp.zeros((8, LANES), jnp.int32)
        for r in range(8):
            mine = jnp.where(sub == r, order[view, g * 8 + r], mine)
        orders.append(mine)
    for l in range(blocks):
        prefix = [ones] * groups
        total = jnp.ones((1, LANES), f32)
        for k in range(slabs):
            other = keep[k // 8 * blocks + l][k % 8 : k % 8 + 1]
            total = total * other
            rank_k = order[view, k]
            for g in range(groups):
                prefix[g] = prefix[g] * jnp.where(rank_k < orders[g], other, 1.0)
        for m in range(3):
            value = jnp.zeros((1, LANES), f32)
            for g in range(groups):
                value = value + jnp.sum(prefix[g] * shade[(g * blocks + l) * 3 + m], axis=0, keepdims=True)
            out[m, :, l * LANES : (l + 1) * LANES] = value
        out[3, :, l * LANES : (l + 1) * LANES] = total


def body(slabs, tiles, centers, scale, angle, opacity, color, rank, dest, order):
    views = centers.shape[1]
    rows = centers.shape[3]
    cap = 2 * rows // tiles
    entries = tiles * cap
    columns = views * PW * PH // slabs
    copies = slabs // views
    direct = cap % LANES == 0
    vmem = pl.BlockSpec(memory_space=pltpu.VMEM)
    smem = pl.BlockSpec(memory_space=pltpu.SMEM)

    out_shape = (slabs * tiles, 1, NF * cap) if direct else (views, NF, entries)
    sent = pl.pallas_call(
        partial(sender_kernel, views, tiles, copies, direct),
        out_shape=jax.ShapeDtypeStruct(out_shape, f32),
        in_specs=[vmem] * 7,
        out_specs=vmem,
        scratch_shapes=[pltpu.VMEM((views, 16, rows), f32)],
        name="sender",
    )(centers, scale, angle, opacity, color, rank, dest[0, :, :, 0])
    if not direct:
        sent = sent.reshape(views, 1, NF, tiles, cap).transpose(0, 1, 3, 2, 4)
        sent = jnp.broadcast_to(sent, (views, copies, tiles, NF, cap)).reshape(slabs * tiles, 1, NF * cap)
    got = lax.all_to_all(sent, ("slab", "tile"), split_axis=0, concat_axis=0, tiled=True)
    if not direct:
        got = got.reshape(slabs, tiles, NF, cap).transpose(2, 0, 1, 3).reshape(NF, slabs, entries)
    return pl.pallas_call(
        partial(receiver_kernel, slabs, tiles, views, direct),
        out_shape=jax.ShapeDtypeStruct((4, 1, columns), f32),
        in_specs=[smem, vmem],
        out_specs=vmem,
        scratch_shapes=[
            pltpu.VMEM((NF, slabs, entries), f32),
            pltpu.VMEM((slabs, 2 * LANES, entries), f32),
            pltpu.VMEM((slabs * entries, LANES), f32),
            pltpu.VMEM((slabs * entries, LANES), f32),
            pltpu.VMEM((LANES, columns), f32),
        ],
        name="receiver",
    )(order, got)


def solution(mesh):
    in_specs = (
        P("slab", None, None, "tile"),
        P("slab", None, None, "tile"),
        P("slab", None, "tile"),
        P("slab", "tile"),
        P("slab", None, "tile"),
        P("slab", None, "tile"),
        P("slab", None, "tile", None),
        P(),
    )
    return jax.shard_map(
        partial(body, mesh.shape["slab"], mesh.shape["tile"]),
        mesh=mesh,
        in_specs=in_specs,
        out_specs=P(None, "tile", "slab"),
        check_vma=False,
    )
```

```python
from functools import partial
import math

import jax
import jax.numpy as jnp
from jax import lax
from jax.experimental import pallas as pl
from jax.experimental.pallas import tpu as pltpu
from jax.sharding import PartitionSpec as P

PW = 64
PH = 32
NF = 10
HALF_LOG2E = 0.5 * math.log2(math.e)
X_MID = 16.0
LANES = 128
ROW = 128
NQ = 27
VALID = 27
COLOR_HI = 28
COLOR_LO = 31
TABLE = 48

f32 = jnp.float32
bf16 = jnp.bfloat16
NT = (((1,), (1,)), ((), ()))


def pieces(x, count):
    out = []
    for _ in range(count):
        part = x.astype(bf16)
        out.append(part)
        x = x - part.astype(f32)
    return out


def sender_kernel(views, tiles, copies, direct, centers, scale, angle, opacity, color, rank, dest, out, feat):
    rows = centers.shape[3]
    cap = 2 * rows // tiles
    slots = tiles * cap
    hot_rows = -(-tiles // 16) * 16

    theta = angle[0]
    cosine = jnp.cos(theta)
    sine = jnp.sin(theta)
    feat[...] = jnp.zeros_like(feat)
    before = lax.broadcasted_iota(jnp.int32, (rows, rows), 0) < lax.broadcasted_iota(jnp.int32, (rows, rows), 1)
    before = jnp.where(before, 1.0, 0.0).astype(bf16)
    tile_id = lax.broadcasted_iota(jnp.int32, (hot_rows, rows), 0)
    slot_id = lax.broadcasted_iota(jnp.int32, (slots, rows), 0)
    for v in range(views):
        s1 = scale[0, v, 0:1]
        s2 = scale[0, v, 1:2]
        i1 = 1.0 / (s1 * s1)
        i2 = 1.0 / (s2 * s2)
        c = cosine[v : v + 1]
        s = sine[v : v + 1]
        feat[v, 0:1] = centers[0, v, 0:1]
        feat[v, 1:2] = centers[0, v, 1:2]
        feat[v, 2:3] = c * c * i1 + s * s * i2
        feat[v, 3:4] = c * s * (i1 - i2)
        feat[v, 4:5] = s * s * i1 + c * c * i2
        feat[v, 5:6] = opacity[0:1]
        for i in range(3):
            feat[v, 6 + i : 7 + i] = color[i]
        feat[v, 9:10] = rank[0, v : v + 1].astype(f32)

        target = dest[0, v]
        hot = jnp.where(tile_id == target, 1.0, 0.0)
        earlier = jnp.dot(hot.astype(bf16), before, preferred_element_type=f32)
        place = jnp.sum(hot * earlier, axis=0, keepdims=True).astype(jnp.int32)
        slot = target * cap + place
        pick = jnp.where(slot_id == slot, 1.0, 0.0).astype(bf16)
        stack = jnp.concatenate(pieces(feat[v], 3), axis=0)
        moved = lax.dot_general(stack, pick, NT, preferred_element_type=f32)
        moved = moved[0:16] + moved[16:32] + moved[32:48]
        if direct:
            for t in range(tiles):
                block = moved[0:NF, t * cap : (t + 1) * cap]
                for q in range(copies):
                    out[pl.ds(((v * copies + q) * tiles + t) * NF, NF), :] = block
        else:
            out[v] = moved[0:NF]


def positions(rank, real, slabs, n_ranks):
    entries = rank.shape[1]
    side = 1 << ((n_ranks - 1).bit_length() + 1) // 2
    together = min(slabs, max(1, 256 // side))
    rows = together * side
    high = jnp.floor(rank * (1.0 / side))
    low = rank - high * side
    high = jnp.where(real, high, 2.0 * side)
    digit = lax.broadcasted_iota(jnp.int32, (rows, entries), 0) % side
    digit = digit.astype(f32)
    same = lax.broadcasted_iota(jnp.int32, (rows, rows), 0) // side
    same = same == lax.broadcasted_iota(jnp.int32, (rows, rows), 1) // side

    def spread(x, k):
        return jnp.concatenate([jnp.broadcast_to(x[k + i : k + i + 1], (side, entries)) for i in range(together)], axis=0)

    def mark(condition):
        return jnp.where(condition, 1.0, 0.0).astype(bf16)

    out = []
    for k in range(0, slabs, together):
        hi = spread(high, k)
        lo = spread(low, k)
        is_hi = hi == digit
        left = jnp.concatenate([mark(is_hi), mark(hi < digit)], axis=1)
        right = jnp.concatenate([mark(lo < digit), jnp.ones((rows, entries), bf16)], axis=1)
        front = lax.dot_general(left, right, NT, preferred_element_type=f32)
        front = jnp.concatenate(pieces(jnp.where(same, front, 0.0), 2), axis=1)
        is_lo = mark(lo == digit)
        mine = jnp.dot(front, jnp.concatenate([is_lo, is_lo], axis=0), preferred_element_type=f32)
        mine = jnp.where(is_hi, mine, 0.0)
        for i in range(together):
            out.append(jnp.sum(mine[i * side : (i + 1) * side], axis=0, keepdims=True))
    return jnp.where(real, jnp.concatenate(out, axis=0), -1.0)


def receiver_kernel(
    slabs, tiles, views, direct, n_ranks, order, recv, out, coef, sorted_rows, basis, q0, q1, w0, w1, em0, em1, acc
):
    entries = coef.shape[0] * LANES
    columns = out.shape[2]
    blocks = columns // LANES
    pixels = PW * PH
    groups = slabs // 8
    chunk = q0.shape[0]
    chunks = slabs * entries // chunk
    shades = 3 * slabs

    me = lax.axis_index("slab")
    first = me * columns
    view = first // pixels
    y_first = (first - view * pixels) // PW
    half_rows = columns // PW // 2
    y_mid = (y_first + half_rows).astype(f32)

    def feature(f):
        if direct:
            return jnp.concatenate(
                [recv[pl.ds(t * NF + f, slabs, stride=tiles * NF), :] for t in range(tiles)], axis=1
            )
        return recv[f]

    o = feature(5)
    real = o > 0.0
    place = positions(feature(9), real, slabs, n_ranks)
    x = feature(0) - X_MID
    y = feature(1) - y_mid
    a = feature(2)
    b = feature(3)
    c = feature(4)
    h = -HALF_LOG2E
    ax_by = a * x + b * y
    bx_cy = b * x + c * y
    constant = h * (x * ax_by + y * bx_cy) + jnp.log2(jnp.where(real, o, 1.0))
    table_rows = []
    for one in (h * a, (2.0 * h) * b, h * c):
        parts = [p.astype(f32) for p in pieces(one, 3)]
        table_rows += parts + parts
    for one in ((-2.0 * h) * ax_by, (-2.0 * h) * bx_cy, constant):
        table_rows += [p.astype(f32) for p in pieces(one, 3)]
    table_rows.append(jnp.ones_like(o))
    colors = [[p.astype(f32) for p in pieces(feature(6 + i), 2)] for i in range(3)]
    table_rows += [p[0] for p in colors] + [p[1] for p in colors]
    table_rows += [jnp.zeros_like(o)] * (TABLE - len(table_rows))
    for i, one in enumerate(table_rows):
        for t in range(entries // LANES):
            coef[t, i * slabs : (i + 1) * slabs, :] = one[:, t * LANES : (t + 1) * LANES]

    lane = lax.broadcasted_iota(jnp.int32, (1, columns), 1)
    row = lane // PW
    u = (lane - row * PW).astype(f32) + (0.5 - X_MID)
    w = (row - half_rows).astype(f32) + 0.5
    basis_rows = []
    for one in (u * u, u * w, w * w):
        hi, lo = pieces(one, 2)
        basis_rows += [hi.astype(f32)] * 3 + [lo.astype(f32)] * 3
    basis_rows += [u] * 3 + [w] * 3 + [jnp.ones_like(u)] * 3 + [jnp.full_like(u, 400.0)]
    basis[...] = jnp.zeros_like(basis)
    for i, one in enumerate(basis_rows):
        basis[i : i + 1] = one
    monomials = basis[...].astype(bf16)

    missing = jnp.where(lax.broadcasted_iota(jnp.int32, (1, ROW), 1) == VALID, -1.0, 0.0)
    want = lax.broadcasted_iota(jnp.int32, (256, entries), 0).astype(f32).astype(bf16)
    zero_rows = jnp.zeros((ROW - TABLE, entries), bf16)
    for k in range(slabs):
        table = [coef[t, pl.ds(k, TABLE, stride=slabs), :] for t in range(entries // LANES)]
        table = jnp.concatenate(table, axis=1).astype(bf16)
        table = jnp.concatenate([table, zero_rows], axis=0)
        for j in range(0, entries, 256):
            mine = jnp.broadcast_to((place[k : k + 1] - j).astype(bf16), (256, entries))
            pick = jnp.where(mine == want, jnp.ones_like(mine), jnp.zeros_like(mine))
            got = lax.dot_general(pick, table, NT, preferred_element_type=f32)
            sorted_rows[pl.ds(j * slabs + k, 256, stride=slabs), :] = got + missing

    which = lax.broadcasted_iota(jnp.int32, (2 * shades, ROW), 0)
    which_lane = lax.broadcasted_iota(jnp.int32, (2 * shades, ROW), 1)
    choose = jnp.where(which // slabs + COLOR_HI == which_lane, 1.0, 0.0).astype(bf16)
    own = lax.broadcasted_iota(jnp.int32, (2 * shades, chunk), 0) % slabs
    own = own == lax.broadcasted_iota(jnp.int32, (2 * shades, chunk), 1) % slabs

    def exponents(i, q, em):
        base = pl.multiple_of(jnp.minimum(i, chunks - 1) * chunk, chunk)
        lhs = sorted_rows[pl.ds(base, chunk), :].astype(bf16)
        q[...] = jnp.dot(lhs, monomials, preferred_element_type=f32)
        picked = lax.dot_general(choose, lhs, NT, preferred_element_type=f32)
        picked = jnp.where(own, picked, 0.0).astype(bf16)
        em[:, 0:chunk] = picked
        em[:, chunk:] = picked

    def weights(q, w, keep):
        keep = list(keep)
        for r in range(0, chunk, 16):
            for l in range(blocks):
                both = []
                for half in range(2):
                    at = r + 8 * half
                    n = at // 8 % groups * blocks + l
                    alpha = jnp.exp2(q[at : at + 8, l * LANES : (l + 1) * LANES])
                    one = alpha * keep[n]
                    keep[n] = keep[n] - one
                    both.append(one)
                both = jnp.concatenate(both, axis=0)
                hi = both.astype(bf16)
                w[r : r + 16, l * LANES : (l + 1) * LANES] = hi
                w[chunk + r : chunk + r + 16, l * LANES : (l + 1) * LANES] = (both - hi.astype(f32)).astype(bf16)
        return tuple(keep)

    def shade(em, w):
        acc[...] += jnp.dot(em[...], w[...], preferred_element_type=f32)

    acc[...] = jnp.zeros_like(acc)
    em1[...] = jnp.zeros_like(em1)
    w1[...] = jnp.zeros_like(w1)
    exponents(0, q0, em0)

    def two_chunks(i, keep):
        shade(em1, w1)
        exponents(2 * i + 1, q1, em1)
        keep = weights(q0, w0, keep)
        shade(em0, w0)
        exponents(2 * i + 2, q0, em0)
        return weights(q1, w1, keep)

    ones = jnp.ones((8, LANES), f32)
    keep = lax.fori_loop(0, chunks // 2, two_chunks, (ones,) * (groups * blocks))
    shade(em1, w1)

    sub = lax.broadcasted_iota(jnp.int32, (8, LANES), 0)
    orders = []
    for g in range(groups):
        mine = jnp.zeros((8, LANES), jnp.int32)
        for r in range(8):
            mine = jnp.where(sub == r, order[view, g * 8 + r], mine)
        orders.append(mine)
    for l in range(blocks):
        at = slice(l * LANES, (l + 1) * LANES)
        prefix = [ones] * groups
        total = jnp.ones((1, LANES), f32)
        for k in range(slabs):
            other = keep[k // 8 * blocks + l][k % 8 : k % 8 + 1]
            total = total * other
            rank_k = order[view, k]
            for g in range(groups):
                prefix[g] = prefix[g] * jnp.where(rank_k < orders[g], other, 1.0)
        for m in range(3):
            value = jnp.zeros((1, LANES), f32)
            for g in range(groups):
                r = m * slabs + g * 8
                value = value + jnp.sum(
                    prefix[g] * (acc[r : r + 8, at] + acc[shades + r : shades + r + 8, at]), axis=0, keepdims=True
                )
            out[m, :, at] = value
        out[3, :, at] = total


def body(slabs, tiles, centers, scale, angle, opacity, color, rank, dest, order):
    views = centers.shape[1]
    rows = centers.shape[3]
    cap = 2 * rows // tiles
    entries = tiles * cap
    columns = views * PW * PH // slabs
    copies = slabs // views
    direct = cap % LANES == 0
    vmem = pl.BlockSpec(memory_space=pltpu.VMEM)
    smem = pl.BlockSpec(memory_space=pltpu.SMEM)

    out_shape = (slabs * tiles * NF, cap) if direct else (views, NF, entries)
    sent = pl.pallas_call(
        partial(sender_kernel, views, tiles, copies, direct),
        out_shape=jax.ShapeDtypeStruct(out_shape, f32),
        in_specs=[vmem] * 7,
        out_specs=vmem,
        scratch_shapes=[pltpu.VMEM((views, 16, rows), f32)],
        name="sender",
    )(centers, scale, angle, opacity, color.transpose(1, 0, 2), rank, dest.transpose(0, 1, 3, 2))
    if not direct:
        sent = sent.reshape(views, 1, NF, tiles, cap).transpose(0, 1, 3, 2, 4)
        sent = jnp.broadcast_to(sent, (views, copies, tiles, NF, cap)).reshape(slabs * tiles, 1, NF * cap)
    sent = sent.reshape(slabs * tiles, 1, NF * cap)
    got = lax.all_to_all(sent, ("slab", "tile"), split_axis=0, concat_axis=0, tiled=True)
    if direct:
        got = got.reshape(slabs * tiles * NF, cap)
    else:
        got = got.reshape(slabs, tiles, NF, cap).transpose(2, 0, 1, 3).reshape(NF, slabs, entries)
    chunk = 256
    width = 6 * slabs
    return pl.pallas_call(
        partial(receiver_kernel, slabs, tiles, views, direct, tiles * rows),
        out_shape=jax.ShapeDtypeStruct((4, 1, columns), f32),
        in_specs=[smem, vmem],
        out_specs=vmem,
        scratch_shapes=[
            pltpu.VMEM((entries // LANES, TABLE * slabs, LANES), f32),
            pltpu.VMEM((slabs * entries, ROW), f32),
            pltpu.VMEM((ROW, columns), f32),
            pltpu.VMEM((chunk, columns), f32),
            pltpu.VMEM((chunk, columns), f32),
            pltpu.VMEM((2 * chunk, columns), bf16),
            pltpu.VMEM((2 * chunk, columns), bf16),
            pltpu.VMEM((width, 2 * chunk), bf16),
            pltpu.VMEM((width, 2 * chunk), bf16),
            pltpu.VMEM((width, columns), f32),
        ],
        name="receiver",
    )(order, got)


def solution(mesh):
    in_specs = (
        P("slab", None, None, "tile"),
        P("slab", None, None, "tile"),
        P("slab", None, "tile"),
        P("slab", "tile"),
        P("slab", None, "tile"),
        P("slab", None, "tile"),
        P("slab", None, "tile", None),
        P(),
    )
    return jax.shard_map(
        partial(body, mesh.shape["slab"], mesh.shape["tile"]),
        mesh=mesh,
        in_specs=in_specs,
        out_specs=P(None, "tile", "slab"),
        check_vma=False,
    )
```

```python
from functools import partial
import math

import jax
import jax.numpy as jnp
from jax import lax
from jax.experimental import pallas as pl
from jax.experimental.pallas import tpu as pltpu
from jax.sharding import PartitionSpec as P

PW = 64
PH = 32
NF = 10
HALF_LOG2E = 0.5 * math.log2(math.e)
X_MID = 16.0
LANES = 128
GROUP = 32
STEPS = 64
VALID = 24
COLOR = 25

f32 = jnp.float32
bf16 = jnp.bfloat16
NT = (((1,), (1,)), ((), ()))


def pieces(x, count):
    out = []
    for _ in range(count):
        part = x.astype(bf16)
        out.append(part)
        x = x - part.astype(f32)
    return out


def sender_kernel(views, tiles, copies, direct, centers, scale, angle, opacity, color, rank, dest, out, feat):
    rows = centers.shape[3]
    cap = 2 * rows // tiles
    slots = tiles * cap
    hot_rows = -(-tiles // 16) * 16

    theta = angle[0]
    cosine = jnp.cos(theta)
    sine = jnp.sin(theta)
    feat[...] = jnp.zeros_like(feat)
    before = lax.broadcasted_iota(jnp.int32, (rows, rows), 0) < lax.broadcasted_iota(jnp.int32, (rows, rows), 1)
    before = jnp.where(before, 1.0, 0.0).astype(bf16)
    tile_id = lax.broadcasted_iota(jnp.int32, (hot_rows, rows), 0)
    slot_id = lax.broadcasted_iota(jnp.int32, (slots, rows), 0)
    for v in range(views):
        s1 = scale[0, v, 0:1]
        s2 = scale[0, v, 1:2]
        i1 = 1.0 / (s1 * s1)
        i2 = 1.0 / (s2 * s2)
        c = cosine[v : v + 1]
        s = sine[v : v + 1]
        feat[v, 0:1] = centers[0, v, 0:1]
        feat[v, 1:2] = centers[0, v, 1:2]
        feat[v, 2:3] = c * c * i1 + s * s * i2
        feat[v, 3:4] = c * s * (i1 - i2)
        feat[v, 4:5] = s * s * i1 + c * c * i2
        feat[v, 5:6] = opacity[0:1]
        for i in range(3):
            feat[v, 6 + i : 7 + i] = color[i]
        feat[v, 9:10] = rank[0, v : v + 1].astype(f32)

        target = dest[0, v]
        hot = jnp.where(tile_id == target, 1.0, 0.0)
        earlier = jnp.dot(hot.astype(bf16), before, preferred_element_type=f32)
        place = jnp.sum(hot * earlier, axis=0, keepdims=True).astype(jnp.int32)
        slot = target * cap + place
        pick = jnp.where(slot_id == slot, 1.0, 0.0).astype(bf16)
        stack = jnp.concatenate(pieces(feat[v], 3), axis=0)
        moved = lax.dot_general(stack, pick, NT, preferred_element_type=f32)
        moved = moved[0:16] + moved[16:32] + moved[32:48]
        if direct:
            for t in range(tiles):
                block = moved[0:NF, t * cap : (t + 1) * cap]
                for q in range(copies):
                    out[pl.ds(((v * copies + q) * tiles + t) * NF, NF), :] = block
        else:
            out[v] = moved[0:NF]


def mark(condition):
    return jnp.where(condition, jnp.ones(condition.shape, bf16), jnp.zeros(condition.shape, bf16))


def positions(rank, real, slabs, n_ranks):
    entries = rank.shape[1]
    side = 1 << ((n_ranks - 1).bit_length() + 1) // 2
    together = min(slabs, max(1, 256 // side))
    rows = together * side
    high = jnp.floor(rank * (1.0 / side))
    low = rank - high * side
    high = jnp.where(real, high, 2.0 * side)
    digit = (lax.broadcasted_iota(jnp.int32, (rows, entries), 0) % side).astype(f32)
    digit_b = digit.astype(bf16)
    same = lax.broadcasted_iota(jnp.int32, (rows, rows), 0) // side
    same = same == lax.broadcasted_iota(jnp.int32, (rows, rows), 1) // side

    def spread(x, k):
        return jnp.concatenate([jnp.broadcast_to(x[k + i : k + i + 1], (side, entries)) for i in range(together)], axis=0)

    out = []
    for k in range(0, slabs, together):
        hi = spread(high.astype(bf16), k)
        lo = spread(low.astype(bf16), k)
        left = jnp.concatenate([mark(hi == digit_b), mark(hi < digit_b)], axis=1)
        right = jnp.concatenate([mark(lo < digit_b), jnp.ones((rows, entries), bf16)], axis=1)
        front = lax.dot_general(left, right, NT, preferred_element_type=f32)
        front = jnp.concatenate(pieces(jnp.where(same, front, 0.0), 2), axis=1)
        is_lo = mark(lo == digit_b)
        mine = jnp.dot(front, jnp.concatenate([is_lo, is_lo], axis=0), preferred_element_type=f32)
        mine = jnp.where(spread(high, k) == digit, mine, 0.0)
        for i in range(together):
            out.append(jnp.sum(mine[i * side : (i + 1) * side], axis=0, keepdims=True))
    return jnp.where(real, jnp.concatenate(out, axis=0), -1.0)


def receiver_kernel(slabs, tiles, views, direct, n_ranks, order, recv, out, coef, lists, basis, q0, q1, w0, w1, acc):
    entries = coef.shape[0] * LANES
    columns = out.shape[2]
    blocks = columns // LANES
    pixels = PW * PH
    groups = slabs // 8
    chunks = entries // STEPS
    per_row = LANES // GROUP
    shades = 3 * slabs

    me = lax.axis_index("slab")
    first = me * columns
    view = first // pixels
    y_first = (first - view * pixels) // PW
    half_rows = columns // PW // 2
    y_mid = (y_first + half_rows).astype(f32)

    def feature(f):
        if direct:
            return jnp.concatenate(
                [recv[pl.ds(t * NF + f, slabs, stride=tiles * NF), :] for t in range(tiles)], axis=1
            )
        return recv[f]

    o = feature(5)
    real = o > 0.0
    place = positions(feature(9), real, slabs, n_ranks)
    x = feature(0) - X_MID
    y = feature(1) - y_mid
    a = feature(2)
    b = feature(3)
    c = feature(4)
    h = -HALF_LOG2E
    ax_by = a * x + b * y
    bx_cy = b * x + c * y
    constant = h * (x * ax_by + y * bx_cy) + jnp.log2(jnp.where(real, o, 1.0))
    table_rows = []
    for one, count in ((h * a, 2), ((2.0 * h) * b, 2), (h * c, 1)):
        table_rows += [p.astype(f32) for p in pieces(one, 3)] * count
    for one in ((-2.0 * h) * ax_by, (-2.0 * h) * bx_cy, constant):
        table_rows += [p.astype(f32) for p in pieces(one, 3)]
    table_rows.append(jnp.ones_like(o))
    colors = [[p.astype(f32) for p in pieces(feature(6 + i), 2)] for i in range(3)]
    table_rows += [p[0] for p in colors] + [p[1] for p in colors]
    table_rows += [jnp.zeros_like(o)] * (GROUP - len(table_rows))
    for i, one in enumerate(table_rows):
        for t in range(entries // LANES):
            coef[t, i * slabs : (i + 1) * slabs, :] = one[:, t * LANES : (t + 1) * LANES]

    lane = lax.broadcasted_iota(jnp.int32, (1, columns), 1)
    row = lane // PW
    u = (lane - row * PW).astype(f32) + (0.5 - X_MID)
    w = (row - half_rows).astype(f32) + 0.5
    basis_rows = []
    for one, count in ((u * u, 2), (u * w, 2), (w * w, 1)):
        for part in pieces(one, count):
            basis_rows += [part.astype(f32)] * 3
    basis_rows += [u] * 3 + [w] * 3 + [jnp.ones_like(u)] * 3 + [jnp.full_like(u, 400.0)]
    basis[...] = jnp.zeros_like(basis)
    for i, one in enumerate(basis_rows):
        basis[LANES - GROUP + i : LANES - GROUP + i + 1] = one

    missing = jnp.where(lax.broadcasted_iota(jnp.int32, (1, chunks * GROUP), 1) % GROUP == VALID, -1.0, 0.0)
    want = lax.broadcasted_iota(jnp.int32, (STEPS, entries), 0).astype(f32).astype(bf16)
    place_group = jnp.floor(place * (1.0 / STEPS))
    place_step = (place - place_group * STEPS).astype(bf16)
    place_group = place_group.astype(bf16)
    for k in range(slabs):
        table = [coef[t, pl.ds(k, GROUP, stride=slabs), :] for t in range(entries // LANES)]
        table = jnp.concatenate(table, axis=1).astype(bf16)
        group = jnp.broadcast_to(place_group[k : k + 1], (GROUP, entries))
        spread = [
            jnp.where(group == jnp.full((GROUP, entries), g, bf16), table, jnp.zeros_like(table)) for g in range(chunks)
        ]
        spread = jnp.concatenate(spread, axis=0)
        pick = mark(jnp.broadcast_to(place_step[k : k + 1], (STEPS, entries)) == want)
        got = lax.dot_general(pick, spread, NT, preferred_element_type=f32) + missing
        for t in range(chunks // per_row):
            lists[t, pl.ds(k, STEPS, stride=slabs), :] = got[:, t * LANES : (t + 1) * LANES]
    sorted_lists = [lists[t].astype(bf16) for t in range(chunks // per_row)]

    shade_rows = []
    for t in range(chunks // per_row):
        r = lax.broadcasted_iota(jnp.int32, (per_row * 8, LANES), 0)
        choose = lax.broadcasted_iota(jnp.int32, (per_row * 8, LANES), 1) == r // 8 * GROUP + COLOR + r % 8
        choose = jnp.where(choose & (r % 8 < 6), 1.0, 0.0).astype(bf16)
        shade_rows.append(lax.dot_general(choose, sorted_lists[t], NT, preferred_element_type=f32))
    own = lax.broadcasted_iota(jnp.int32, (slabs, STEPS * slabs), 0)
    own = own == lax.broadcasted_iota(jnp.int32, (slabs, STEPS * slabs), 1) % slabs

    def exponents(g, q):
        first_row = LANES - GROUP - g % per_row * GROUP
        monomials = basis[first_row : first_row + LANES].astype(bf16)
        q[...] = jnp.dot(sorted_lists[g // per_row], monomials, preferred_element_type=f32)

    def weights(q, w, keep):
        keep = list(keep)
        for r in range(0, STEPS * slabs, 8):
            for l in range(blocks):
                n = r // 8 % groups * blocks + l
                one = jnp.exp2(q[r : r + 8, l * LANES : (l + 1) * LANES]) * keep[n]
                keep[n] = keep[n] - one
                w[r : r + 8, l * LANES : (l + 1) * LANES] = one
        return keep

    def shade(g, w):
        rows = [
            jnp.where(own, shade_rows[g // per_row][g % per_row * 8 + i : g % per_row * 8 + i + 1], 0.0)
            for i in range(6)
        ]
        rows = jnp.concatenate(rows, axis=0).astype(bf16)
        hi, lo = pieces(w[...], 2)
        return jnp.dot(
            jnp.concatenate([rows, rows], axis=1), jnp.concatenate([hi, lo], axis=0), preferred_element_type=f32
        )

    ones = jnp.ones((8, LANES), f32)
    keep = [ones] * (groups * blocks)
    exponents(0, q0)
    for g in range(chunks):
        if g + 1 < chunks:
            exponents(g + 1, (q0, q1)[(g + 1) % 2])
        keep = weights((q0, q1)[g % 2], (w0, w1)[g % 2], keep)
        part = shade(g, (w0, w1)[g % 2])
        acc[...] = part if g == 0 else acc[...] + part

    sub = lax.broadcasted_iota(jnp.int32, (8, LANES), 0)
    orders = []
    for g in range(groups):
        mine = jnp.zeros((8, LANES), jnp.int32)
        for r in range(8):
            mine = jnp.where(sub == r, order[view, g * 8 + r], mine)
        orders.append(mine)
    for l in range(blocks):
        at = slice(l * LANES, (l + 1) * LANES)
        prefix = [ones] * groups
        total = jnp.ones((1, LANES), f32)
        for k in range(slabs):
            other = keep[k // 8 * blocks + l][k % 8 : k % 8 + 1]
            total = total * other
            rank_k = order[view, k]
            for g in range(groups):
                prefix[g] = prefix[g] * jnp.where(rank_k < orders[g], other, 1.0)
        for m in range(3):
            value = jnp.zeros((1, LANES), f32)
            for g in range(groups):
                r = m * slabs + g * 8
                value = value + jnp.sum(
                    prefix[g] * (acc[r : r + 8, at] + acc[shades + r : shades + r + 8, at]), axis=0, keepdims=True
                )
            out[m, :, at] = value
        out[3, :, at] = total


def body(slabs, tiles, centers, scale, angle, opacity, color, rank, dest, order):
    views = centers.shape[1]
    rows = centers.shape[3]
    cap = 2 * rows // tiles
    entries = tiles * cap
    columns = views * PW * PH // slabs
    copies = slabs // views
    direct = cap % LANES == 0
    vmem = pl.BlockSpec(memory_space=pltpu.VMEM)
    smem = pl.BlockSpec(memory_space=pltpu.SMEM)

    out_shape = (slabs * tiles * NF, cap) if direct else (views, NF, entries)
    sent = pl.pallas_call(
        partial(sender_kernel, views, tiles, copies, direct),
        out_shape=jax.ShapeDtypeStruct(out_shape, f32),
        in_specs=[vmem] * 7,
        out_specs=vmem,
        scratch_shapes=[pltpu.VMEM((views, 16, rows), f32)],
        name="sender",
    )(centers, scale, angle, opacity, color.transpose(1, 0, 2), rank, dest.transpose(0, 1, 3, 2))
    if not direct:
        sent = sent.reshape(views, 1, NF, tiles, cap).transpose(0, 1, 3, 2, 4)
        sent = jnp.broadcast_to(sent, (views, copies, tiles, NF, cap)).reshape(slabs * tiles, 1, NF * cap)
    sent = sent.reshape(slabs * tiles, 1, NF * cap)
    got = lax.all_to_all(sent, ("slab", "tile"), split_axis=0, concat_axis=0, tiled=True)
    if direct:
        got = got.reshape(slabs * tiles * NF, cap)
    else:
        got = got.reshape(slabs, tiles, NF, cap).transpose(2, 0, 1, 3).reshape(NF, slabs, entries)
    lanes = entries // STEPS * GROUP
    return pl.pallas_call(
        partial(receiver_kernel, slabs, tiles, views, direct, tiles * rows),
        out_shape=jax.ShapeDtypeStruct((4, 1, columns), f32),
        in_specs=[smem, vmem],
        out_specs=vmem,
        scratch_shapes=[
            pltpu.VMEM((entries // LANES, GROUP * slabs, LANES), f32),
            pltpu.VMEM((lanes // LANES, STEPS * slabs, LANES), f32),
            pltpu.VMEM((2 * LANES - GROUP, columns), f32),
            pltpu.VMEM((STEPS * slabs, columns), f32),
            pltpu.VMEM((STEPS * slabs, columns), f32),
            pltpu.VMEM((STEPS * slabs, columns), f32),
            pltpu.VMEM((STEPS * slabs, columns), f32),
            pltpu.VMEM((6 * slabs, columns), f32),
        ],
        name="receiver",
    )(order, got)


def solution(mesh):
    in_specs = (
        P("slab", None, None, "tile"),
        P("slab", None, None, "tile"),
        P("slab", None, "tile"),
        P("slab", "tile"),
        P("slab", None, "tile"),
        P("slab", None, "tile"),
        P("slab", None, "tile", None),
        P(),
    )
    return jax.shard_map(
        partial(body, mesh.shape["slab"], mesh.shape["tile"]),
        mesh=mesh,
        in_specs=in_specs,
        out_specs=P(None, "tile", "slab"),
        check_vma=False,
    )
```

```python
from functools import partial
import math

import jax
import jax.numpy as jnp
from jax import lax
from jax.experimental import pallas as pl
from jax.experimental.pallas import tpu as pltpu
from jax.sharding import PartitionSpec as P

PW = 64
PH = 32
NF = 10
HALF_LOG2E = 0.5 * math.log2(math.e)
X_MID = 16.0
LANES = 128
GROUP = 32
STEPS = 64
VALID = 24
COLOR = 25

f32 = jnp.float32
bf16 = jnp.bfloat16
NT = (((1,), (1,)), ((), ()))


def pieces(x, count):
    out = []
    for _ in range(count):
        part = x.astype(bf16)
        out.append(part)
        x = x - part.astype(f32)
    return out


def sender_kernel(views, tiles, copies, direct, centers, scale, angle, opacity, color, rank, dest, out, feat):
    rows = centers.shape[3]
    cap = 2 * rows // tiles
    slots = tiles * cap
    hot_rows = -(-tiles // 16) * 16

    theta = angle[0]
    cosine = jnp.cos(theta)
    sine = jnp.sin(theta)
    feat[...] = jnp.zeros_like(feat)
    before = lax.broadcasted_iota(jnp.int32, (rows, rows), 0) < lax.broadcasted_iota(jnp.int32, (rows, rows), 1)
    before = jnp.where(before, 1.0, 0.0).astype(bf16)
    tile_id = lax.broadcasted_iota(jnp.int32, (hot_rows, rows), 0)
    slot_id = lax.broadcasted_iota(jnp.int32, (slots, rows), 0)
    for v in range(views):
        s1 = scale[0, v, 0:1]
        s2 = scale[0, v, 1:2]
        i1 = 1.0 / (s1 * s1)
        i2 = 1.0 / (s2 * s2)
        c = cosine[v : v + 1]
        s = sine[v : v + 1]
        feat[v, 0:1] = centers[0, v, 0:1]
        feat[v, 1:2] = centers[0, v, 1:2]
        feat[v, 2:3] = c * c * i1 + s * s * i2
        feat[v, 3:4] = c * s * (i1 - i2)
        feat[v, 4:5] = s * s * i1 + c * c * i2
        feat[v, 5:6] = opacity[0:1]
        for i in range(3):
            feat[v, 6 + i : 7 + i] = color[i]
        feat[v, 9:10] = rank[0, v : v + 1].astype(f32)

        target = dest[0, v]
        hot = jnp.where(tile_id == target, 1.0, 0.0)
        earlier = jnp.dot(hot.astype(bf16), before, preferred_element_type=f32)
        place = jnp.sum(hot * earlier, axis=0, keepdims=True).astype(jnp.int32)
        slot = target * cap + place
        pick = jnp.where(slot_id == slot, 1.0, 0.0).astype(bf16)
        stack = jnp.concatenate(pieces(feat[v], 3), axis=0)
        moved = lax.dot_general(stack, pick, NT, preferred_element_type=f32)
        moved = moved[0:16] + moved[16:32] + moved[32:48]
        if direct:
            for t in range(tiles):
                block = moved[0:NF, t * cap : (t + 1) * cap]
                for q in range(copies):
                    out[pl.ds(((v * copies + q) * tiles + t) * NF, NF), :] = block
        else:
            out[v] = moved[0:NF]


def mark(condition):
    return jnp.where(condition, jnp.ones(condition.shape, bf16), jnp.zeros(condition.shape, bf16))


def positions(rank, real, slabs, n_ranks):
    entries = rank.shape[1]
    tall = 16
    wide = -(-n_ranks // tall)
    high = jnp.floor(rank * (1.0 / wide))
    low = (rank - high * wide).astype(bf16)
    high = jnp.where(real, high, 2.0 * tall)
    high_b = high.astype(bf16)
    tall_f = lax.broadcasted_iota(jnp.int32, (tall, entries), 0).astype(f32)
    tall_b = tall_f.astype(bf16)
    wide_b = lax.broadcasted_iota(jnp.int32, (wide, entries), 0).astype(f32).astype(bf16)
    ones = jnp.ones((wide, entries), bf16)

    fronts = []
    for k in range(slabs):
        hi = jnp.broadcast_to(high_b[k : k + 1], (tall, entries))
        lo = jnp.broadcast_to(low[k : k + 1], (wide, entries))
        left = jnp.concatenate([mark(hi == tall_b), mark(hi < tall_b)], axis=1)
        right = jnp.concatenate([mark(lo < wide_b), ones], axis=1)
        front = lax.dot_general(left, right, NT, preferred_element_type=f32)
        fronts.append(jnp.concatenate(pieces(front, 2), axis=1))
    out = []
    for k in range(slabs):
        is_lo = mark(jnp.broadcast_to(low[k : k + 1], (wide, entries)) == wide_b)
        mine = jnp.dot(fronts[k], jnp.concatenate([is_lo, is_lo], axis=0), preferred_element_type=f32)
        mine = jnp.where(high[k : k + 1] == tall_f, mine, 0.0)
        out.append(jnp.sum(mine, axis=0, keepdims=True))
    return jnp.where(real, jnp.concatenate(out, axis=0), -1.0)


def receiver_kernel(slabs, tiles, views, direct, n_ranks, order_hbm, recv, out, coef, lists, basis, q0, q1, w0, w1, acc, order, order_sem):
    entries = coef.shape[0] * LANES
    columns = out.shape[2]
    blocks = columns // LANES
    pixels = PW * PH
    groups = slabs // 8
    chunks = entries // STEPS
    per_row = LANES // GROUP
    shades = 3 * slabs

    fetch = pltpu.make_async_copy(order_hbm, order, order_sem)
    fetch.start()
    me = lax.axis_index("slab")
    first = me * columns
    view = first // pixels
    y_first = (first - view * pixels) // PW
    half_rows = columns // PW // 2
    y_mid = (y_first + half_rows).astype(f32)

    def feature(f):
        if direct:
            return jnp.concatenate(
                [recv[pl.ds(t * NF + f, slabs, stride=tiles * NF), :] for t in range(tiles)], axis=1
            )
        return recv[f]

    o = feature(5)
    real = o > 0.0
    place = positions(feature(9), real, slabs, n_ranks)
    x = feature(0) - X_MID
    y = feature(1) - y_mid
    a = feature(2)
    b = feature(3)
    c = feature(4)
    h = -HALF_LOG2E
    ax_by = a * x + b * y
    bx_cy = b * x + c * y
    constant = h * (x * ax_by + y * bx_cy) + jnp.log2(jnp.where(real, o, 1.0))
    table_rows = []
    for one, count in ((h * a, 2), ((2.0 * h) * b, 2), (h * c, 1)):
        table_rows += [p.astype(f32) for p in pieces(one, 3)] * count
    for one in ((-2.0 * h) * ax_by, (-2.0 * h) * bx_cy, constant):
        table_rows += [p.astype(f32) for p in pieces(one, 3)]
    table_rows.append(jnp.ones_like(o))
    colors = [[p.astype(f32) for p in pieces(feature(6 + i), 2)] for i in range(3)]
    table_rows += [p[0] for p in colors] + [p[1] for p in colors]
    table_rows += [jnp.zeros_like(o)] * (GROUP - len(table_rows))
    for i, one in enumerate(table_rows):
        for t in range(entries // LANES):
            coef[t, i * slabs : (i + 1) * slabs, :] = one[:, t * LANES : (t + 1) * LANES]

    lane = lax.broadcasted_iota(jnp.int32, (1, columns), 1)
    row = lane // PW
    u = (lane - row * PW).astype(f32) + (0.5 - X_MID)
    w = (row - half_rows).astype(f32) + 0.5
    basis_rows = []
    for one, count in ((u * u, 2), (u * w, 2), (w * w, 1)):
        for part in pieces(one, count):
            basis_rows += [part.astype(f32)] * 3
    basis_rows += [u] * 3 + [w] * 3 + [jnp.ones_like(u)] * 3 + [jnp.full_like(u, 400.0)]
    basis[...] = jnp.zeros_like(basis)
    for i, one in enumerate(basis_rows):
        basis[LANES - GROUP + i : LANES - GROUP + i + 1] = one

    missing = jnp.where(lax.broadcasted_iota(jnp.int32, (1, chunks * GROUP), 1) % GROUP == VALID, -1.0, 0.0)
    want = lax.broadcasted_iota(jnp.int32, (STEPS, entries), 0).astype(f32).astype(bf16)
    place_group = jnp.floor(place * (1.0 / STEPS))
    place_step = (place - place_group * STEPS).astype(bf16)
    place_group = place_group.astype(bf16)
    for k in range(slabs):
        table = [coef[t, pl.ds(k, GROUP, stride=slabs), :] for t in range(entries // LANES)]
        table = jnp.concatenate(table, axis=1).astype(bf16)
        group = jnp.broadcast_to(place_group[k : k + 1], (GROUP, entries))
        spread = [
            jnp.where(group == jnp.full((GROUP, entries), g, bf16), table, jnp.zeros_like(table)) for g in range(chunks)
        ]
        spread = jnp.concatenate(spread, axis=0)
        pick = mark(jnp.broadcast_to(place_step[k : k + 1], (STEPS, entries)) == want)
        got = lax.dot_general(pick, spread, NT, preferred_element_type=f32) + missing
        for t in range(chunks // per_row):
            lists[t, pl.ds(k, STEPS, stride=slabs), :] = got[:, t * LANES : (t + 1) * LANES]
    sorted_lists = [lists[t].astype(bf16) for t in range(chunks // per_row)]

    shade_rows = []
    for t in range(chunks // per_row):
        r = lax.broadcasted_iota(jnp.int32, (per_row * 8, LANES), 0)
        choose = lax.broadcasted_iota(jnp.int32, (per_row * 8, LANES), 1) == r // 8 * GROUP + COLOR + r % 8
        choose = jnp.where(choose & (r % 8 < 6), 1.0, 0.0).astype(bf16)
        shade_rows.append(lax.dot_general(choose, sorted_lists[t], NT, preferred_element_type=f32))
    own = lax.broadcasted_iota(jnp.int32, (slabs, STEPS * slabs), 0)
    own = own == lax.broadcasted_iota(jnp.int32, (slabs, STEPS * slabs), 1) % slabs

    def exponents(g, q):
        first_row = LANES - GROUP - g % per_row * GROUP
        monomials = basis[first_row : first_row + LANES].astype(bf16)
        q[...] = jnp.dot(sorted_lists[g // per_row], monomials, preferred_element_type=f32)

    def weights(q, w, keep):
        keep = list(keep)
        for r in range(0, STEPS * slabs, 8):
            for l in range(blocks):
                n = r // 8 % groups * blocks + l
                one = jnp.exp2(q[r : r + 8, l * LANES : (l + 1) * LANES]) * keep[n]
                keep[n] = keep[n] - one
                w[r : r + 8, l * LANES : (l + 1) * LANES] = one
        return keep

    def shade(g, w):
        rows = [
            jnp.where(own, shade_rows[g // per_row][g % per_row * 8 + i : g % per_row * 8 + i + 1], 0.0)
            for i in range(6)
        ]
        rows = jnp.concatenate(rows, axis=0).astype(bf16)
        hi, lo = pieces(w[...], 2)
        return jnp.dot(
            jnp.concatenate([rows, rows], axis=1), jnp.concatenate([hi, lo], axis=0), preferred_element_type=f32
        )

    ones = jnp.ones((8, LANES), f32)
    keep = [ones] * (groups * blocks)
    exponents(0, q0)
    for g in range(chunks):
        if g + 1 < chunks:
            exponents(g + 1, (q0, q1)[(g + 1) % 2])
        keep = weights((q0, q1)[g % 2], (w0, w1)[g % 2], keep)
        part = shade(g, (w0, w1)[g % 2])
        acc[...] = part if g == 0 else acc[...] + part

    fetch.wait()
    sub = lax.broadcasted_iota(jnp.int32, (8, LANES), 0)
    orders = []
    for g in range(groups):
        mine = jnp.zeros((8, LANES), jnp.int32)
        for r in range(8):
            mine = jnp.where(sub == r, order[view, g * 8 + r], mine)
        orders.append(mine)
    for l in range(blocks):
        at = slice(l * LANES, (l + 1) * LANES)
        prefix = [ones] * groups
        total = jnp.ones((1, LANES), f32)
        for k in range(slabs):
            other = keep[k // 8 * blocks + l][k % 8 : k % 8 + 1]
            total = total * other
            rank_k = order[view, k]
            for g in range(groups):
                prefix[g] = prefix[g] * jnp.where(rank_k < orders[g], other, 1.0)
        for m in range(3):
            value = jnp.zeros((1, LANES), f32)
            for g in range(groups):
                r = m * slabs + g * 8
                value = value + jnp.sum(
                    prefix[g] * (acc[r : r + 8, at] + acc[shades + r : shades + r + 8, at]), axis=0, keepdims=True
                )
            out[m, :, at] = value
        out[3, :, at] = total


def body(slabs, tiles, centers, scale, angle, opacity, color, rank, dest, order):
    views = centers.shape[1]
    rows = centers.shape[3]
    cap = 2 * rows // tiles
    entries = tiles * cap
    columns = views * PW * PH // slabs
    copies = slabs // views
    direct = cap % LANES == 0
    vmem = pl.BlockSpec(memory_space=pltpu.VMEM)

    out_shape = (slabs * tiles * NF, cap) if direct else (views, NF, entries)
    sent = pl.pallas_call(
        partial(sender_kernel, views, tiles, copies, direct),
        out_shape=pltpu.VMEM(out_shape, f32),
        in_specs=[vmem] * 7,
        out_specs=vmem,
        scratch_shapes=[pltpu.VMEM((views, 16, rows), f32)],
        name="sender",
    )(centers, scale, angle, opacity, color.transpose(1, 0, 2), rank, dest.transpose(0, 1, 3, 2))
    if not direct:
        sent = sent.reshape(views, 1, NF, tiles, cap).transpose(0, 1, 3, 2, 4)
        sent = jnp.broadcast_to(sent, (views, copies, tiles, NF, cap)).reshape(slabs * tiles, 1, NF * cap)
    sent = sent.reshape(slabs * tiles, 1, NF * cap)
    got = lax.all_to_all(sent, ("slab", "tile"), split_axis=0, concat_axis=0, tiled=True)
    if direct:
        got = got.reshape(slabs * tiles * NF, cap)
    else:
        got = got.reshape(slabs, tiles, NF, cap).transpose(2, 0, 1, 3).reshape(NF, slabs, entries)
    lanes = entries // STEPS * GROUP
    return pl.pallas_call(
        partial(receiver_kernel, slabs, tiles, views, direct, tiles * rows),
        out_shape=jax.ShapeDtypeStruct((4, 1, columns), f32),
        in_specs=[pl.BlockSpec(memory_space=pl.ANY), vmem],
        out_specs=vmem,
        scratch_shapes=[
            pltpu.VMEM((entries // LANES, GROUP * slabs, LANES), f32),
            pltpu.VMEM((lanes // LANES, STEPS * slabs, LANES), f32),
            pltpu.VMEM((2 * LANES - GROUP, columns), f32),
            pltpu.VMEM((STEPS * slabs, columns), f32),
            pltpu.VMEM((STEPS * slabs, columns), f32),
            pltpu.VMEM((STEPS * slabs, columns), f32),
            pltpu.VMEM((STEPS * slabs, columns), f32),
            pltpu.VMEM((6 * slabs, columns), f32),
            pltpu.SMEM(order.shape, jnp.int32),
            pltpu.SemaphoreType.DMA,
        ],
        name="receiver",
    )(order, pltpu.with_memory_space_constraint(got, pltpu.VMEM))


def solution(mesh):
    in_specs = (
        P("slab", None, None, "tile"),
        P("slab", None, None, "tile"),
        P("slab", None, "tile"),
        P("slab", "tile"),
        P("slab", None, "tile"),
        P("slab", None, "tile"),
        P("slab", None, "tile", None),
        P(),
    )
    return jax.shard_map(
        partial(body, mesh.shape["slab"], mesh.shape["tile"]),
        mesh=mesh,
        in_specs=in_specs,
        out_specs=P(None, "tile", "slab"),
        check_vma=False,
    )
```

```python
from functools import partial
import math

import jax
import jax.numpy as jnp
from jax import lax
from jax.experimental import pallas as pl
from jax.experimental.pallas import tpu as pltpu
from jax.sharding import PartitionSpec as P

PW = 64
PH = 32
NF = 10
HALF_LOG2E = 0.5 * math.log2(math.e)
X_MID = 16.0
LANES = 128
GROUP = 32
PART = 16
AHEAD = 2
LAG = 2
STEPS = 128
VALID = 24
COLOR = 25

f32 = jnp.float32
bf16 = jnp.bfloat16
NT = (((1,), (1,)), ((), ()))


def pieces(x, count):
    out = []
    for _ in range(count):
        part = x.astype(bf16)
        out.append(part)
        x = x - part.astype(f32)
    return out


def sender_kernel(views, tiles, copies, direct, centers, scale, angle, opacity, color, rank, dest, out, feat):
    rows = centers.shape[3]
    cap = 2 * rows // tiles
    slots = tiles * cap
    hot_rows = -(-tiles // 16) * 16

    theta = angle[0]
    cosine = jnp.cos(theta)
    sine = jnp.sin(theta)
    feat[...] = jnp.zeros_like(feat)
    before = lax.broadcasted_iota(jnp.int32, (rows, rows), 0) < lax.broadcasted_iota(jnp.int32, (rows, rows), 1)
    before = jnp.where(before, 1.0, 0.0).astype(bf16)
    tile_id = lax.broadcasted_iota(jnp.int32, (hot_rows, rows), 0)
    slot_id = lax.broadcasted_iota(jnp.int32, (slots, rows), 0)
    for v in range(views):
        s1 = scale[0, v, 0:1]
        s2 = scale[0, v, 1:2]
        i1 = 1.0 / (s1 * s1)
        i2 = 1.0 / (s2 * s2)
        c = cosine[v : v + 1]
        s = sine[v : v + 1]
        feat[v, 0:1] = centers[0, v, 0:1]
        feat[v, 1:2] = centers[0, v, 1:2]
        feat[v, 2:3] = c * c * i1 + s * s * i2
        feat[v, 3:4] = c * s * (i1 - i2)
        feat[v, 4:5] = s * s * i1 + c * c * i2
        feat[v, 5:6] = opacity[0:1]
        for i in range(3):
            feat[v, 6 + i : 7 + i] = color[i]
        feat[v, 9:10] = rank[0, v : v + 1].astype(f32)

        target = dest[0, v]
        hot = jnp.where(tile_id == target, 1.0, 0.0)
        earlier = jnp.dot(hot.astype(bf16), before, preferred_element_type=f32)
        place = jnp.sum(hot * earlier, axis=0, keepdims=True).astype(jnp.int32)
        slot = target * cap + place
        pick = jnp.where(slot_id == slot, 1.0, 0.0).astype(bf16)
        stack = jnp.concatenate(pieces(feat[v], 3), axis=0)
        moved = lax.dot_general(stack, pick, NT, preferred_element_type=f32)
        moved = moved[0:16] + moved[16:32] + moved[32:48]
        if direct:
            for t in range(tiles):
                block = moved[0:NF, t * cap : (t + 1) * cap]
                for q in range(copies):
                    out[pl.ds(((v * copies + q) * tiles + t) * NF, NF), :] = block
        else:
            out[v] = moved[0:NF]


def mark(condition):
    return jnp.where(condition, jnp.ones(condition.shape, bf16), jnp.zeros(condition.shape, bf16))


def positions(rank, real, slabs, n_ranks):
    entries = rank.shape[1]
    tall = 32
    wide = -(-n_ranks // tall)
    high = jnp.floor(rank * (1.0 / wide))
    low = (rank - high * wide).astype(bf16)
    high = jnp.where(real, high, 2.0 * tall)
    high_b = high.astype(bf16)
    tall_f = lax.broadcasted_iota(jnp.int32, (tall, entries), 0).astype(f32)
    tall_b = tall_f.astype(bf16)
    wide_b = lax.broadcasted_iota(jnp.int32, (wide, entries), 0).astype(f32).astype(bf16)
    ones = jnp.ones((wide, entries), bf16)

    fronts = []
    for k in range(slabs):
        hi = jnp.broadcast_to(high_b[k : k + 1], (tall, entries))
        lo = jnp.broadcast_to(low[k : k + 1], (wide, entries))
        left = jnp.concatenate([mark(hi == tall_b), mark(hi < tall_b)], axis=1)
        right = jnp.concatenate([mark(lo < wide_b), ones], axis=1)
        front = lax.dot_general(left, right, NT, preferred_element_type=f32)
        fronts.append(jnp.concatenate(pieces(front, 2), axis=1))
    out = []
    for k in range(slabs):
        is_lo = mark(jnp.broadcast_to(low[k : k + 1], (wide, entries)) == wide_b)
        mine = jnp.dot(fronts[k], jnp.concatenate([is_lo, is_lo], axis=0), preferred_element_type=f32)
        mine = jnp.where(high[k : k + 1] == tall_f, mine, 0.0)
        out.append(jnp.sum(mine, axis=0, keepdims=True))
    return jnp.where(real, jnp.concatenate(out, axis=0), -1.0)


def receiver_kernel(slabs, tiles, views, direct, n_ranks, order_hbm, recv, out, coef, lists, basis, acc, order, order_sem):
    entries = coef.shape[0] * LANES
    columns = out.shape[2]
    blocks = columns // LANES
    pixels = PW * PH
    groups = slabs // 8
    chunks = entries // STEPS
    per_row = LANES // GROUP
    shades = 3 * slabs

    fetch = pltpu.make_async_copy(order_hbm, order, order_sem)
    fetch.start()
    me = lax.axis_index("slab")
    first = me * columns
    view = first // pixels
    y_first = (first - view * pixels) // PW
    half_rows = columns // PW // 2
    y_mid = (y_first + half_rows).astype(f32)

    def feature(f):
        if direct:
            return jnp.concatenate(
                [recv[pl.ds(t * NF + f, slabs, stride=tiles * NF), :] for t in range(tiles)], axis=1
            )
        return recv[f]

    o = feature(5)
    real = o > 0.0
    place = positions(feature(9), real, slabs, n_ranks)
    x = feature(0) - X_MID
    y = feature(1) - y_mid
    a = feature(2)
    b = feature(3)
    c = feature(4)
    h = -HALF_LOG2E
    ax_by = a * x + b * y
    bx_cy = b * x + c * y
    constant = h * (x * ax_by + y * bx_cy) + jnp.log2(jnp.where(real, o, 1.0))
    table_rows = []
    for one, count in ((h * a, 2), ((2.0 * h) * b, 2), (h * c, 1)):
        table_rows += [p.astype(f32) for p in pieces(one, 3)] * count
    for one in ((-2.0 * h) * ax_by, (-2.0 * h) * bx_cy, constant):
        table_rows += [p.astype(f32) for p in pieces(one, 3)]
    table_rows.append(jnp.ones_like(o))
    colors = [[p.astype(f32) for p in pieces(feature(6 + i), 2)] for i in range(3)]
    table_rows += [p[0] for p in colors] + [p[1] for p in colors]
    table_rows += [jnp.zeros_like(o)] * (GROUP - len(table_rows))
    for i, one in enumerate(table_rows):
        for t in range(entries // LANES):
            coef[t, i * slabs : (i + 1) * slabs, :] = one[:, t * LANES : (t + 1) * LANES]

    lane = lax.broadcasted_iota(jnp.int32, (1, columns), 1)
    row = lane // PW
    u = (lane - row * PW).astype(f32) + (0.5 - X_MID)
    w = (row - half_rows).astype(f32) + 0.5
    basis_rows = []
    for one, count in ((u * u, 2), (u * w, 2), (w * w, 1)):
        for part in pieces(one, count):
            basis_rows += [part.astype(f32)] * 3
    basis_rows += [u] * 3 + [w] * 3 + [jnp.ones_like(u)] * 3 + [jnp.full_like(u, 400.0)]
    basis[...] = jnp.zeros_like(basis)
    for i, one in enumerate(basis_rows):
        basis[LANES - GROUP + i : LANES - GROUP + i + 1] = one

    missing = jnp.where(lax.broadcasted_iota(jnp.int32, (1, chunks * GROUP), 1) % GROUP == VALID, -1.0, 0.0)
    want = lax.broadcasted_iota(jnp.int32, (STEPS, entries), 0).astype(f32).astype(bf16)
    place_group = jnp.floor(place * (1.0 / STEPS))
    place_step = (place - place_group * STEPS).astype(bf16)
    place_group = place_group.astype(bf16)
    for k in range(slabs):
        table = [coef[t, pl.ds(k, GROUP, stride=slabs), :] for t in range(entries // LANES)]
        table = jnp.concatenate(table, axis=1).astype(bf16)
        group = jnp.broadcast_to(place_group[k : k + 1], (GROUP, entries))
        spread = [
            jnp.where(group == jnp.full((GROUP, entries), g, bf16), table, jnp.zeros_like(table)) for g in range(chunks)
        ]
        spread = jnp.concatenate(spread, axis=0)
        pick = mark(jnp.broadcast_to(place_step[k : k + 1], (STEPS, entries)) == want)
        got = lax.dot_general(pick, spread, NT, preferred_element_type=f32) + missing
        for t in range(chunks // per_row):
            lists[t, pl.ds(k, STEPS, stride=slabs), :] = got[:, t * LANES : (t + 1) * LANES]
    sorted_lists = [lists[t].astype(bf16) for t in range(chunks // per_row)]

    shade_rows = []
    for t in range(chunks // per_row):
        r = lax.broadcasted_iota(jnp.int32, (per_row * 8, LANES), 0)
        choose = lax.broadcasted_iota(jnp.int32, (per_row * 8, LANES), 1) == r // 8 * GROUP + COLOR + r % 8
        choose = jnp.where(choose & (r % 8 < 6), 1.0, 0.0).astype(bf16)
        shade_rows.append(lax.dot_general(choose, sorted_lists[t], NT, preferred_element_type=f32))
    own = lax.broadcasted_iota(jnp.int32, (slabs, PART * slabs), 0)
    own = own == lax.broadcasted_iota(jnp.int32, (slabs, PART * slabs), 1) % slabs

    rows = PART * slabs
    per_chunk = STEPS // PART

    def exponents(n):
        g, p = n // per_chunk, n % per_chunk
        first_row = LANES - GROUP - g % per_row * GROUP
        monomials = basis[first_row : first_row + LANES].astype(bf16)
        lhs = sorted_lists[g // per_row][p * rows : (p + 1) * rows]
        return jnp.dot(lhs, monomials, preferred_element_type=f32)

    def weights(q, keep):
        highs = []
        lows = []
        for r in range(0, rows, 16):
            hi_row = []
            lo_row = []
            for l in range(blocks):
                both = []
                for at in (r, r + 8):
                    i = at // 8 % groups * blocks + l
                    one = jnp.exp2(q[at : at + 8, l * LANES : (l + 1) * LANES]) * keep[i]
                    keep[i] = keep[i] - one
                    both.append(one)
                hi, lo = pieces(jnp.concatenate(both, axis=0), 2)
                hi_row.append(hi)
                lo_row.append(lo)
            highs.append(jnp.concatenate(hi_row, axis=1))
            lows.append(jnp.concatenate(lo_row, axis=1))
        return jnp.concatenate(highs + lows, axis=0)

    def colours(n):
        g, p = n // per_chunk, n % per_chunk
        some = shade_rows[g // per_row][g % per_row * 8 : g % per_row * 8 + 8, p * rows : (p + 1) * rows]
        some = [jnp.where(own, some[i : i + 1], 0.0) for i in range(6)]
        some = jnp.concatenate(some, axis=0).astype(bf16)
        return jnp.concatenate([some, some], axis=1)

    ones = jnp.ones((8, LANES), f32)
    keep = [ones] * (groups * blocks)
    total = jnp.zeros((6 * slabs, columns), f32)
    parts = chunks * per_chunk
    ahead = [exponents(n) for n in range(AHEAD)]
    behind = []
    for n in range(parts + LAG):
        if n >= LAG:
            total = total + jnp.dot(colours(n - LAG), behind.pop(0), preferred_element_type=f32)
        if n + AHEAD < parts:
            ahead.append(exponents(n + AHEAD))
        if n < parts:
            behind.append(weights(ahead.pop(0), keep))
    acc[...] = total

    fetch.wait()
    sub = lax.broadcasted_iota(jnp.int32, (8, LANES), 0)
    orders = []
    for g in range(groups):
        mine = jnp.zeros((8, LANES), jnp.int32)
        for r in range(8):
            mine = jnp.where(sub == r, order[view, g * 8 + r], mine)
        orders.append(mine)
    for l in range(blocks):
        at = slice(l * LANES, (l + 1) * LANES)
        prefix = [ones] * groups
        total = jnp.ones((1, LANES), f32)
        for k in range(slabs):
            other = keep[k // 8 * blocks + l][k % 8 : k % 8 + 1]
            total = total * other
            rank_k = order[view, k]
            for g in range(groups):
                prefix[g] = prefix[g] * jnp.where(rank_k < orders[g], other, 1.0)
        for m in range(3):
            value = jnp.zeros((1, LANES), f32)
            for g in range(groups):
                r = m * slabs + g * 8
                value = value + jnp.sum(
                    prefix[g] * (acc[r : r + 8, at] + acc[shades + r : shades + r + 8, at]), axis=0, keepdims=True
                )
            out[m, :, at] = value
        out[3, :, at] = total


def body(slabs, tiles, centers, scale, angle, opacity, color, rank, dest, order):
    views = centers.shape[1]
    rows = centers.shape[3]
    cap = 2 * rows // tiles
    entries = tiles * cap
    columns = views * PW * PH // slabs
    copies = slabs // views
    direct = cap % LANES == 0
    vmem = pl.BlockSpec(memory_space=pltpu.VMEM)

    out_shape = (slabs * tiles * NF, cap) if direct else (views, NF, entries)
    sent = pl.pallas_call(
        partial(sender_kernel, views, tiles, copies, direct),
        out_shape=pltpu.VMEM(out_shape, f32),
        in_specs=[vmem] * 7,
        out_specs=vmem,
        scratch_shapes=[pltpu.VMEM((views, 16, rows), f32)],
        name="sender",
    )(centers, scale, angle, opacity, color.transpose(1, 0, 2), rank, dest.transpose(0, 1, 3, 2))
    if not direct:
        sent = sent.reshape(views, 1, NF, tiles, cap).transpose(0, 1, 3, 2, 4)
        sent = jnp.broadcast_to(sent, (views, copies, tiles, NF, cap)).reshape(slabs * tiles, 1, NF * cap)
    sent = sent.reshape(slabs * tiles, 1, NF * cap)
    got = lax.all_to_all(sent, ("slab", "tile"), split_axis=0, concat_axis=0, tiled=True)
    if direct:
        got = got.reshape(slabs * tiles * NF, cap)
    else:
        got = got.reshape(slabs, tiles, NF, cap).transpose(2, 0, 1, 3).reshape(NF, slabs, entries)
    lanes = entries // STEPS * GROUP
    return pl.pallas_call(
        partial(receiver_kernel, slabs, tiles, views, direct, tiles * rows),
        out_shape=jax.ShapeDtypeStruct((4, 1, columns), f32),
        in_specs=[pl.BlockSpec(memory_space=pl.ANY), vmem],
        out_specs=vmem,
        scratch_shapes=[
            pltpu.VMEM((entries // LANES, GROUP * slabs, LANES), f32),
            pltpu.VMEM((lanes // LANES, STEPS * slabs, LANES), f32),
            pltpu.VMEM((2 * LANES - GROUP, columns), f32),
            pltpu.VMEM((6 * slabs, columns), f32),
            pltpu.SMEM(order.shape, jnp.int32),
            pltpu.SemaphoreType.DMA,
        ],
        name="receiver",
    )(order, pltpu.with_memory_space_constraint(got, pltpu.VMEM))


def solution(mesh):
    in_specs = (
        P("slab", None, None, "tile"),
        P("slab", None, None, "tile"),
        P("slab", None, "tile"),
        P("slab", "tile"),
        P("slab", None, "tile"),
        P("slab", None, "tile"),
        P("slab", None, "tile", None),
        P(),
    )
    return jax.shard_map(
        partial(body, mesh.shape["slab"], mesh.shape["tile"]),
        mesh=mesh,
        in_specs=in_specs,
        out_specs=P(None, "tile", "slab"),
        check_vma=False,
    )
```

```python
from functools import partial
import math

import jax
import jax.numpy as jnp
from jax import lax
from jax.experimental import pallas as pl
from jax.experimental.pallas import tpu as pltpu
from jax.sharding import PartitionSpec as P

PW = 64
PH = 32
NF = 10
HALF_LOG2E = 0.5 * math.log2(math.e)
X_MID = 16.0
LANES = 128
GROUP = 32
PART = 16
AHEAD = 2
LAG = 2
STOPS = (5, 6, 7, 8, 9, 16)
STEPS = 128
VALID = 24
COLOR = 25

f32 = jnp.float32
bf16 = jnp.bfloat16
NT = (((1,), (1,)), ((), ()))


def pieces(x, count):
    out = []
    for _ in range(count):
        part = x.astype(bf16)
        out.append(part)
        x = x - part.astype(f32)
    return out


def sender_kernel(views, tiles, copies, direct, centers, scale, angle, opacity, color, rank, dest, out, feat):
    rows = centers.shape[3]
    cap = 2 * rows // tiles
    slots = tiles * cap
    hot_rows = -(-tiles // 16) * 16

    theta = angle[0]
    cosine = jnp.cos(theta)
    sine = jnp.sin(theta)
    feat[...] = jnp.zeros_like(feat)
    before = lax.broadcasted_iota(jnp.int32, (rows, rows), 0) < lax.broadcasted_iota(jnp.int32, (rows, rows), 1)
    before = jnp.where(before, 1.0, 0.0).astype(bf16)
    tile_id = lax.broadcasted_iota(jnp.int32, (hot_rows, rows), 0)
    slot_id = lax.broadcasted_iota(jnp.int32, (slots, rows), 0)
    for v in range(views):
        s1 = scale[0, v, 0:1]
        s2 = scale[0, v, 1:2]
        i1 = 1.0 / (s1 * s1)
        i2 = 1.0 / (s2 * s2)
        c = cosine[v : v + 1]
        s = sine[v : v + 1]
        feat[v, 0:1] = centers[0, v, 0:1]
        feat[v, 1:2] = centers[0, v, 1:2]
        feat[v, 2:3] = c * c * i1 + s * s * i2
        feat[v, 3:4] = c * s * (i1 - i2)
        feat[v, 4:5] = s * s * i1 + c * c * i2
        feat[v, 5:6] = opacity[0:1]
        for i in range(3):
            feat[v, 6 + i : 7 + i] = color[i]
        feat[v, 9:10] = rank[0, v : v + 1].astype(f32)

        target = dest[0, v]
        hot = jnp.where(tile_id == target, 1.0, 0.0)
        earlier = jnp.dot(hot.astype(bf16), before, preferred_element_type=f32)
        place = jnp.sum(hot * earlier, axis=0, keepdims=True).astype(jnp.int32)
        slot = target * cap + place
        pick = jnp.where(slot_id == slot, 1.0, 0.0).astype(bf16)
        stack = jnp.concatenate(pieces(feat[v], 3), axis=0)
        moved = lax.dot_general(stack, pick, NT, preferred_element_type=f32)
        moved = moved[0:16] + moved[16:32] + moved[32:48]
        if direct:
            for t in range(tiles):
                block = moved[0:NF, t * cap : (t + 1) * cap]
                for q in range(copies):
                    out[pl.ds(((v * copies + q) * tiles + t) * NF, NF), :] = block
        else:
            out[v] = moved[0:NF]


def mark(condition):
    return jnp.where(condition, jnp.ones(condition.shape, bf16), jnp.zeros(condition.shape, bf16))


def positions(rank, real, slabs, n_ranks):
    entries = rank.shape[1]
    tall = 32
    wide = -(-n_ranks // tall)
    high = jnp.floor(rank * (1.0 / wide))
    low = (rank - high * wide).astype(bf16)
    high = jnp.where(real, high, 2.0 * tall)
    high_b = high.astype(bf16)
    tall_f = lax.broadcasted_iota(jnp.int32, (tall, entries), 0).astype(f32)
    tall_b = tall_f.astype(bf16)
    wide_b = lax.broadcasted_iota(jnp.int32, (wide, entries), 0).astype(f32).astype(bf16)
    ones = jnp.ones((wide, entries), bf16)

    fronts = []
    for k in range(slabs):
        hi = jnp.broadcast_to(high_b[k : k + 1], (tall, entries))
        lo = jnp.broadcast_to(low[k : k + 1], (wide, entries))
        left = jnp.concatenate([mark(hi == tall_b), mark(hi < tall_b)], axis=1)
        right = jnp.concatenate([mark(lo < wide_b), ones], axis=1)
        front = lax.dot_general(left, right, NT, preferred_element_type=f32)
        fronts.append(jnp.concatenate(pieces(front, 2), axis=1))
    out = []
    for k in range(slabs):
        is_lo = mark(jnp.broadcast_to(low[k : k + 1], (wide, entries)) == wide_b)
        mine = jnp.dot(fronts[k], jnp.concatenate([is_lo, is_lo], axis=0), preferred_element_type=f32)
        mine = jnp.where(high[k : k + 1] == tall_f, mine, 0.0)
        out.append(jnp.sum(mine, axis=0, keepdims=True))
    return jnp.where(real, jnp.concatenate(out, axis=0), -1.0)


def receiver_kernel(slabs, tiles, views, direct, n_ranks, order_hbm, recv, out, coef, lists, basis, acc, kept, order, order_sem):
    entries = coef.shape[0] * LANES
    columns = out.shape[2]
    blocks = columns // LANES
    pixels = PW * PH
    groups = slabs // 8
    chunks = entries // STEPS
    per_row = LANES // GROUP
    shades = 3 * slabs

    fetch = pltpu.make_async_copy(order_hbm, order, order_sem)
    fetch.start()
    me = lax.axis_index("slab")
    first = me * columns
    view = first // pixels
    y_first = (first - view * pixels) // PW
    half_rows = columns // PW // 2
    y_mid = (y_first + half_rows).astype(f32)

    def feature(f):
        if direct:
            return jnp.concatenate(
                [recv[pl.ds(t * NF + f, slabs, stride=tiles * NF), :] for t in range(tiles)], axis=1
            )
        return recv[f]

    o = feature(5)
    real = o > 0.0
    longest = jnp.max(jnp.sum(jnp.where(real, 1.0, 0.0), axis=1))
    place = positions(feature(9), real, slabs, n_ranks)
    x = feature(0) - X_MID
    y = feature(1) - y_mid
    a = feature(2)
    b = feature(3)
    c = feature(4)
    h = -HALF_LOG2E
    ax_by = a * x + b * y
    bx_cy = b * x + c * y
    constant = h * (x * ax_by + y * bx_cy) + jnp.log2(jnp.where(real, o, 1.0))
    table_rows = []
    for one, count in ((h * a, 2), ((2.0 * h) * b, 2), (h * c, 1)):
        table_rows += [p.astype(f32) for p in pieces(one, 3)] * count
    for one in ((-2.0 * h) * ax_by, (-2.0 * h) * bx_cy, constant):
        table_rows += [p.astype(f32) for p in pieces(one, 3)]
    table_rows.append(jnp.ones_like(o))
    colors = [[p.astype(f32) for p in pieces(feature(6 + i), 2)] for i in range(3)]
    table_rows += [p[0] for p in colors] + [p[1] for p in colors]
    table_rows += [jnp.zeros_like(o)] * (GROUP - len(table_rows))
    for i, one in enumerate(table_rows):
        for t in range(entries // LANES):
            coef[t, i * slabs : (i + 1) * slabs, :] = one[:, t * LANES : (t + 1) * LANES]

    lane = lax.broadcasted_iota(jnp.int32, (1, columns), 1)
    row = lane // PW
    u = (lane - row * PW).astype(f32) + (0.5 - X_MID)
    w = (row - half_rows).astype(f32) + 0.5
    basis_rows = []
    for one, count in ((u * u, 2), (u * w, 2), (w * w, 1)):
        for part in pieces(one, count):
            basis_rows += [part.astype(f32)] * 3
    basis_rows += [u] * 3 + [w] * 3 + [jnp.ones_like(u)] * 3 + [jnp.full_like(u, 400.0)]
    basis[...] = jnp.zeros_like(basis)
    for i, one in enumerate(basis_rows):
        basis[LANES - GROUP + i : LANES - GROUP + i + 1] = one

    missing = jnp.where(lax.broadcasted_iota(jnp.int32, (1, chunks * GROUP), 1) % GROUP == VALID, -1.0, 0.0)
    want = lax.broadcasted_iota(jnp.int32, (STEPS, entries), 0).astype(f32).astype(bf16)
    place_group = jnp.floor(place * (1.0 / STEPS))
    place_step = (place - place_group * STEPS).astype(bf16)
    place_group = place_group.astype(bf16)
    for k in range(slabs):
        table = [coef[t, pl.ds(k, GROUP, stride=slabs), :] for t in range(entries // LANES)]
        table = jnp.concatenate(table, axis=1).astype(bf16)
        group = jnp.broadcast_to(place_group[k : k + 1], (GROUP, entries))
        spread = [
            jnp.where(group == jnp.full((GROUP, entries), g, bf16), table, jnp.zeros_like(table)) for g in range(chunks)
        ]
        spread = jnp.concatenate(spread, axis=0)
        pick = mark(jnp.broadcast_to(place_step[k : k + 1], (STEPS, entries)) == want)
        got = lax.dot_general(pick, spread, NT, preferred_element_type=f32) + missing
        for t in range(chunks // per_row):
            lists[t, pl.ds(k, STEPS, stride=slabs), :] = got[:, t * LANES : (t + 1) * LANES]

    own = lax.broadcasted_iota(jnp.int32, (slabs, PART * slabs), 0)
    own = own == lax.broadcasted_iota(jnp.int32, (slabs, PART * slabs), 1) % slabs

    rows = PART * slabs
    per_chunk = STEPS // PART

    parts = chunks * per_chunk
    ones = jnp.ones((8, LANES), f32)

    def exponents(sorted_lists, n):
        g, p = n // per_chunk, n % per_chunk
        first_row = LANES - GROUP - g % per_row * GROUP
        monomials = basis[first_row : first_row + LANES].astype(bf16)
        lhs = sorted_lists[g // per_row][p * rows : (p + 1) * rows]
        return jnp.dot(lhs, monomials, preferred_element_type=f32)

    def weights(q, keep):
        highs = []
        lows = []
        for r in range(0, rows, 16):
            hi_row = []
            lo_row = []
            for l in range(blocks):
                both = []
                for at in (r, r + 8):
                    i = at // 8 % groups * blocks + l
                    one = jnp.exp2(q[at : at + 8, l * LANES : (l + 1) * LANES]) * keep[i]
                    keep[i] = keep[i] - one
                    both.append(one)
                hi, lo = pieces(jnp.concatenate(both, axis=0), 2)
                hi_row.append(hi)
                lo_row.append(lo)
            highs.append(jnp.concatenate(hi_row, axis=1))
            lows.append(jnp.concatenate(lo_row, axis=1))
        return jnp.concatenate(highs + lows, axis=0)

    def colours(shade_rows, n):
        g, p = n // per_chunk, n % per_chunk
        some = shade_rows[g // per_row][g % per_row * 8 : g % per_row * 8 + 8, p * rows : (p + 1) * rows]
        some = [jnp.where(own, some[i : i + 1], 0.0) for i in range(6)]
        some = jnp.concatenate(some, axis=0).astype(bf16)
        return jnp.concatenate([some, some], axis=1)

    def blend(parts):
        sorted_lists = [lists[t].astype(bf16) for t in range(chunks // per_row)]
        keep = [ones] * (groups * blocks)
        total = jnp.zeros((6 * slabs, columns), f32)
        ahead = [exponents(sorted_lists, n) for n in range(AHEAD)]
        shade_rows = []
        for t in range(chunks // per_row):
            r = lax.broadcasted_iota(jnp.int32, (per_row * 8, LANES), 0)
            choose = lax.broadcasted_iota(jnp.int32, (per_row * 8, LANES), 1) == r // 8 * GROUP + COLOR + r % 8
            choose = jnp.where(choose & (r % 8 < 6), 1.0, 0.0).astype(bf16)
            shade_rows.append(lax.dot_general(choose, sorted_lists[t], NT, preferred_element_type=f32))

        behind = []
        for n in range(parts + LAG):
            if n >= LAG:
                total = total + jnp.dot(colours(shade_rows, n - LAG), behind.pop(0), preferred_element_type=f32)
            if n + AHEAD < parts:
                ahead.append(exponents(sorted_lists, n + AHEAD))
            if n < parts:
                behind.append(weights(ahead.pop(0), keep))
        acc[...] = total
        for i, one in enumerate(keep):
            kept[i] = one

    floor = -1
    for sixteenths in STOPS:
        most = parts * sixteenths // 16
        fits = (longest > floor * PART) & (longest <= most * PART)
        pl.when(fits)(partial(blend, most))
        floor = most
    keep = [kept[i] for i in range(groups * blocks)]

    fetch.wait()
    sub = lax.broadcasted_iota(jnp.int32, (8, LANES), 0)
    orders = []
    for g in range(groups):
        mine = jnp.zeros((8, LANES), jnp.int32)
        for r in range(8):
            mine = jnp.where(sub == r, order[view, g * 8 + r], mine)
        orders.append(mine)
    for l in range(blocks):
        at = slice(l * LANES, (l + 1) * LANES)
        prefix = [ones] * groups
        total = jnp.ones((1, LANES), f32)
        for k in range(slabs):
            other = keep[k // 8 * blocks + l][k % 8 : k % 8 + 1]
            total = total * other
            rank_k = order[view, k]
            for g in range(groups):
                prefix[g] = prefix[g] * jnp.where(rank_k < orders[g], other, 1.0)
        for m in range(3):
            value = jnp.zeros((1, LANES), f32)
            for g in range(groups):
                r = m * slabs + g * 8
                value = value + jnp.sum(
                    prefix[g] * (acc[r : r + 8, at] + acc[shades + r : shades + r + 8, at]), axis=0, keepdims=True
                )
            out[m, :, at] = value
        out[3, :, at] = total


def body(slabs, tiles, centers, scale, angle, opacity, color, rank, dest, order):
    views = centers.shape[1]
    rows = centers.shape[3]
    cap = 2 * rows // tiles
    entries = tiles * cap
    columns = views * PW * PH // slabs
    copies = slabs // views
    direct = cap % LANES == 0
    vmem = pl.BlockSpec(memory_space=pltpu.VMEM)

    out_shape = (slabs * tiles * NF, cap) if direct else (views, NF, entries)
    sent = pl.pallas_call(
        partial(sender_kernel, views, tiles, copies, direct),
        out_shape=pltpu.VMEM(out_shape, f32),
        in_specs=[vmem] * 7,
        out_specs=vmem,
        scratch_shapes=[pltpu.VMEM((views, 16, rows), f32)],
        name="sender",
    )(centers, scale, angle, opacity, color.transpose(1, 0, 2), rank, dest.transpose(0, 1, 3, 2))
    if not direct:
        sent = sent.reshape(views, 1, NF, tiles, cap).transpose(0, 1, 3, 2, 4)
        sent = jnp.broadcast_to(sent, (views, copies, tiles, NF, cap)).reshape(slabs * tiles, 1, NF * cap)
    sent = sent.reshape(slabs * tiles, 1, NF * cap)
    got = lax.all_to_all(sent, ("slab", "tile"), split_axis=0, concat_axis=0, tiled=True)
    if direct:
        got = got.reshape(slabs * tiles * NF, cap)
    else:
        got = got.reshape(slabs, tiles, NF, cap).transpose(2, 0, 1, 3).reshape(NF, slabs, entries)
    lanes = entries // STEPS * GROUP
    return pl.pallas_call(
        partial(receiver_kernel, slabs, tiles, views, direct, tiles * rows),
        out_shape=jax.ShapeDtypeStruct((4, 1, columns), f32),
        in_specs=[pl.BlockSpec(memory_space=pl.ANY), vmem],
        out_specs=vmem,
        scratch_shapes=[
            pltpu.VMEM((entries // LANES, GROUP * slabs, LANES), f32),
            pltpu.VMEM((lanes // LANES, STEPS * slabs, LANES), f32),
            pltpu.VMEM((2 * LANES - GROUP, columns), f32),
            pltpu.VMEM((6 * slabs, columns), f32),
            pltpu.VMEM((slabs // 8 * columns // LANES, 8, LANES), f32),
            pltpu.SMEM(order.shape, jnp.int32),
            pltpu.SemaphoreType.DMA,
        ],
        name="receiver",
    )(order, pltpu.with_memory_space_constraint(got, pltpu.VMEM))


def solution(mesh):
    in_specs = (
        P("slab", None, None, "tile"),
        P("slab", None, None, "tile"),
        P("slab", None, "tile"),
        P("slab", "tile"),
        P("slab", None, "tile"),
        P("slab", None, "tile"),
        P("slab", None, "tile", None),
        P(),
    )
    return jax.shard_map(
        partial(body, mesh.shape["slab"], mesh.shape["tile"]),
        mesh=mesh,
        in_specs=in_specs,
        out_specs=P(None, "tile", "slab"),
        check_vma=False,
    )
```

```python
from functools import partial
import math

import jax
import jax.numpy as jnp
from jax import lax
from jax.experimental import pallas as pl
from jax.experimental.pallas import tpu as pltpu
from jax.sharding import PartitionSpec as P

PW = 64
PH = 32
NF = 10
HALF_LOG2E = 0.5 * math.log2(math.e)
X_MID = 16.0
LANES = 128
GROUP = 32
PART = 16
AHEAD = 2
LAG = 2
STOPS = (5, 6, 7, 8, 9, 16)
STEPS = 128
VALID = 24
COLOR = 25

f32 = jnp.float32
bf16 = jnp.bfloat16
NT = (((1,), (1,)), ((), ()))


def pieces(x, count):
    out = []
    for _ in range(count):
        part = x.astype(bf16)
        out.append(part)
        x = x - part.astype(f32)
    return out


def mark(condition):
    return jnp.where(condition, jnp.ones(condition.shape, bf16), jnp.zeros(condition.shape, bf16))


def sender_kernel(views, tiles, copies, direct, centers, scale, angle, opacity, color, rank, dest, out, feat):
    rows = centers.shape[3]
    cap = 2 * rows // tiles
    slots = tiles * cap
    hot_rows = -(-tiles // 16) * 16

    theta = angle[0]
    cosine = jnp.cos(theta)
    sine = jnp.sin(theta)
    feat[...] = jnp.zeros_like(feat)
    def count_up(shape, axis):
        return lax.broadcasted_iota(jnp.int32, shape, axis).astype(f32).astype(bf16)

    before = mark(count_up((rows, rows), 0) < count_up((rows, rows), 1))
    tile_id = lax.broadcasted_iota(jnp.int32, (hot_rows, rows), 0)
    slot_id = count_up((cap, rows), 0)
    hot = [jnp.where(tile_id == dest[0, v], 1.0, 0.0) for v in range(views)]
    hot = jnp.concatenate(hot, axis=0)
    earlier = hot * jnp.dot(hot.astype(bf16), before, preferred_element_type=f32)
    for v in range(views):
        feat[v, 0:2] = centers[0, v]
        s1 = scale[0, v, 0:1]
        s2 = scale[0, v, 1:2]
        i1 = 1.0 / (s1 * s1)
        i2 = 1.0 / (s2 * s2)
        c = cosine[v : v + 1]
        s = sine[v : v + 1]
        feat[v, 2:3] = c * c * i1 + s * s * i2
        feat[v, 3:4] = c * s * (i1 - i2)
        feat[v, 4:5] = s * s * i1 + c * c * i2
        feat[v, 5:6] = opacity[0:1]
        for i in range(3):
            feat[v, 6 + i : 7 + i] = color[i]
        feat[v, 9:10] = rank[0, v : v + 1].astype(f32)
    for v in range(views):
        place = jnp.sum(earlier[v * hot_rows : (v + 1) * hot_rows], axis=0, keepdims=True)
        slot = dest[0, v].astype(f32) * cap + place
        pick = [mark(jnp.broadcast_to((slot - t * cap).astype(bf16), (cap, rows)) == slot_id) for t in range(tiles)]
        pick = jnp.concatenate(pick, axis=0)
        stack = jnp.concatenate(pieces(feat[v], 3), axis=0)
        moved = lax.dot_general(stack, pick, NT, preferred_element_type=f32)
        moved = moved[0:16] + moved[16:32] + moved[32:48]
        if direct:
            for t in range(tiles):
                block = moved[0:NF, t * cap : (t + 1) * cap]
                for q in range(copies):
                    out[pl.ds(((v * copies + q) * tiles + t) * NF, NF), :] = block
        else:
            out[v] = moved[0:NF]


def positions(rank, real, slabs, n_ranks):
    entries = rank.shape[1]
    tall = 32
    wide = -(-n_ranks // tall)
    high = jnp.floor(rank * (1.0 / wide))
    low = (rank - high * wide).astype(bf16)
    high = jnp.where(real, high, 2.0 * tall)
    high_b = high.astype(bf16)
    tall_f = lax.broadcasted_iota(jnp.int32, (tall, entries), 0).astype(f32)
    tall_b = tall_f.astype(bf16)
    wide_b = lax.broadcasted_iota(jnp.int32, (wide, entries), 0).astype(f32).astype(bf16)
    ones = jnp.ones((wide, entries), bf16)

    fronts = []
    for k in range(slabs):
        hi = jnp.broadcast_to(high_b[k : k + 1], (tall, entries))
        lo = jnp.broadcast_to(low[k : k + 1], (wide, entries))
        left = jnp.concatenate([mark(hi == tall_b), mark(hi < tall_b)], axis=1)
        right = jnp.concatenate([mark(lo < wide_b), ones], axis=1)
        front = lax.dot_general(left, right, NT, preferred_element_type=f32)
        fronts.append(jnp.concatenate(pieces(front, 2), axis=1))
    out = []
    for k in range(slabs):
        is_lo = mark(jnp.broadcast_to(low[k : k + 1], (wide, entries)) == wide_b)
        mine = jnp.dot(fronts[k], jnp.concatenate([is_lo, is_lo], axis=0), preferred_element_type=f32)
        mine = jnp.where(high[k : k + 1] == tall_f, mine, 0.0)
        out.append(jnp.sum(mine, axis=0, keepdims=True))
    return jnp.where(real, jnp.concatenate(out, axis=0), -1.0)


def receiver_kernel(slabs, tiles, views, direct, n_ranks, order_hbm, recv, out, coef, lists, basis, acc, kept, order, order_sem):
    entries = coef.shape[0] * LANES
    columns = out.shape[2]
    blocks = columns // LANES
    pixels = PW * PH
    groups = slabs // 8
    chunks = entries // STEPS
    per_row = LANES // GROUP
    shades = 3 * slabs

    fetch = pltpu.make_async_copy(order_hbm, order, order_sem)
    fetch.start()
    me = lax.axis_index("slab")
    first = me * columns
    view = first // pixels
    y_first = (first - view * pixels) // PW
    half_rows = columns // PW // 2
    y_mid = (y_first + half_rows).astype(f32)

    def feature(f):
        if direct:
            return jnp.concatenate(
                [recv[pl.ds(t * NF + f, slabs, stride=tiles * NF), :] for t in range(tiles)], axis=1
            )
        return recv[f]

    o = feature(5)
    real = o > 0.0
    longest = jnp.max(jnp.sum(jnp.where(real, 1.0, 0.0), axis=1))
    place = positions(feature(9), real, slabs, n_ranks)
    x = feature(0) - X_MID
    y = feature(1) - y_mid
    a = feature(2)
    b = feature(3)
    c = feature(4)
    h = -HALF_LOG2E
    ax_by = a * x + b * y
    bx_cy = b * x + c * y
    constant = h * (x * ax_by + y * bx_cy) + jnp.log2(jnp.where(real, o, 1.0))
    table_rows = []
    for one, count in ((h * a, 2), ((2.0 * h) * b, 2), (h * c, 1)):
        table_rows += [p.astype(f32) for p in pieces(one, 3)] * count
    for one in ((-2.0 * h) * ax_by, (-2.0 * h) * bx_cy, constant):
        table_rows += [p.astype(f32) for p in pieces(one, 3)]
    table_rows.append(jnp.ones_like(o))
    colors = [[p.astype(f32) for p in pieces(feature(6 + i), 2)] for i in range(3)]
    table_rows += [p[0] for p in colors] + [p[1] for p in colors]
    table_rows += [jnp.zeros_like(o)] * (GROUP - len(table_rows))
    for i, one in enumerate(table_rows):
        for t in range(entries // LANES):
            coef[t, i * slabs : (i + 1) * slabs, :] = one[:, t * LANES : (t + 1) * LANES]

    lane = lax.broadcasted_iota(jnp.int32, (1, columns), 1)
    row = lane // PW
    u = (lane - row * PW).astype(f32) + (0.5 - X_MID)
    w = (row - half_rows).astype(f32) + 0.5
    basis_rows = []
    for one, count in ((u * u, 2), (u * w, 2), (w * w, 1)):
        for part in pieces(one, count):
            basis_rows += [part.astype(f32)] * 3
    basis_rows += [u] * 3 + [w] * 3 + [jnp.ones_like(u)] * 3 + [jnp.full_like(u, 400.0)]
    basis[...] = jnp.zeros_like(basis)
    for i, one in enumerate(basis_rows):
        basis[LANES - GROUP + i : LANES - GROUP + i + 1] = one

    missing = jnp.where(lax.broadcasted_iota(jnp.int32, (1, chunks * GROUP), 1) % GROUP == VALID, -1.0, 0.0)
    want = lax.broadcasted_iota(jnp.int32, (STEPS, entries), 0).astype(f32).astype(bf16)
    place_group = jnp.floor(place * (1.0 / STEPS))
    place_step = (place - place_group * STEPS).astype(bf16)
    place_group = place_group.astype(bf16)
    for k in range(slabs):
        table = [coef[t, pl.ds(k, GROUP, stride=slabs), :] for t in range(entries // LANES)]
        table = jnp.concatenate(table, axis=1).astype(bf16)
        group = jnp.broadcast_to(place_group[k : k + 1], (GROUP, entries))
        spread = [
            jnp.where(group == jnp.full((GROUP, entries), g, bf16), table, jnp.zeros_like(table)) for g in range(chunks)
        ]
        spread = jnp.concatenate(spread, axis=0)
        pick = mark(jnp.broadcast_to(place_step[k : k + 1], (STEPS, entries)) == want)
        got = lax.dot_general(pick, spread, NT, preferred_element_type=f32) + missing
        for t in range(chunks // per_row):
            lists[t, pl.ds(k, STEPS, stride=slabs), :] = got[:, t * LANES : (t + 1) * LANES]

    own = lax.broadcasted_iota(jnp.int32, (slabs, PART * slabs), 0)
    own = own == lax.broadcasted_iota(jnp.int32, (slabs, PART * slabs), 1) % slabs

    rows = PART * slabs
    per_chunk = STEPS // PART

    parts = chunks * per_chunk
    ones = jnp.ones((8, LANES), f32)

    def exponents(sorted_lists, n):
        g, p = n // per_chunk, n % per_chunk
        first_row = LANES - GROUP - g % per_row * GROUP
        monomials = basis[first_row : first_row + LANES].astype(bf16)
        lhs = sorted_lists[g // per_row][p * rows : (p + 1) * rows]
        return jnp.dot(lhs, monomials, preferred_element_type=f32)

    def weights(q, keep):
        highs = []
        lows = []
        for r in range(0, rows, 16):
            hi_row = []
            lo_row = []
            for l in range(blocks):
                both = []
                for at in (r, r + 8):
                    i = at // 8 % groups * blocks + l
                    one = jnp.exp2(q[at : at + 8, l * LANES : (l + 1) * LANES]) * keep[i]
                    keep[i] = keep[i] - one
                    both.append(one)
                hi, lo = pieces(jnp.concatenate(both, axis=0), 2)
                hi_row.append(hi)
                lo_row.append(lo)
            highs.append(jnp.concatenate(hi_row, axis=1))
            lows.append(jnp.concatenate(lo_row, axis=1))
        return jnp.concatenate(highs + lows, axis=0)

    def colours(shade_rows, n):
        g, p = n // per_chunk, n % per_chunk
        some = shade_rows[g // per_row][g % per_row * 8 : g % per_row * 8 + 8, p * rows : (p + 1) * rows]
        some = [jnp.where(own, some[i : i + 1], 0.0) for i in range(6)]
        some = jnp.concatenate(some, axis=0).astype(bf16)
        return jnp.concatenate([some, some], axis=1)

    def blend(parts):
        sorted_lists = [lists[t].astype(bf16) for t in range(chunks // per_row)]
        keep = [ones] * (groups * blocks)
        total = jnp.zeros((6 * slabs, columns), f32)
        ahead = [exponents(sorted_lists, n) for n in range(AHEAD)]
        shade_rows = []
        for t in range(chunks // per_row):
            r = lax.broadcasted_iota(jnp.int32, (per_row * 8, LANES), 0)
            choose = lax.broadcasted_iota(jnp.int32, (per_row * 8, LANES), 1) == r // 8 * GROUP + COLOR + r % 8
            choose = jnp.where(choose & (r % 8 < 6), 1.0, 0.0).astype(bf16)
            shade_rows.append(lax.dot_general(choose, sorted_lists[t], NT, preferred_element_type=f32))

        behind = []
        for n in range(parts + LAG):
            if n >= LAG:
                total = total + jnp.dot(colours(shade_rows, n - LAG), behind.pop(0), preferred_element_type=f32)
            if n + AHEAD < parts:
                ahead.append(exponents(sorted_lists, n + AHEAD))
            if n < parts:
                behind.append(weights(ahead.pop(0), keep))
        acc[...] = total
        for i, one in enumerate(keep):
            kept[i] = one

    floor = -1
    for sixteenths in STOPS:
        most = parts * sixteenths // 16
        fits = (longest > floor * PART) & (longest <= most * PART)
        pl.when(fits)(partial(blend, most))
        floor = most
    keep = [kept[i] for i in range(groups * blocks)]

    fetch.wait()
    sub = lax.broadcasted_iota(jnp.int32, (8, LANES), 0)
    orders = []
    for g in range(groups):
        mine = jnp.zeros((8, LANES), jnp.int32)
        for r in range(8):
            mine = jnp.where(sub == r, order[view, g * 8 + r], mine)
        orders.append(mine)
    for l in range(blocks):
        at = slice(l * LANES, (l + 1) * LANES)
        prefix = [ones] * groups
        total = jnp.ones((1, LANES), f32)
        for k in range(slabs):
            other = keep[k // 8 * blocks + l][k % 8 : k % 8 + 1]
            total = total * other
            rank_k = order[view, k]
            for g in range(groups):
                prefix[g] = prefix[g] * jnp.where(rank_k < orders[g], other, 1.0)
        for m in range(3):
            value = jnp.zeros((1, LANES), f32)
            for g in range(groups):
                r = m * slabs + g * 8
                value = value + jnp.sum(
                    prefix[g] * (acc[r : r + 8, at] + acc[shades + r : shades + r + 8, at]), axis=0, keepdims=True
                )
            out[m, :, at] = value
        out[3, :, at] = total


def body(slabs, tiles, centers, scale, angle, opacity, color, rank, dest, order):
    views = centers.shape[1]
    rows = centers.shape[3]
    cap = 2 * rows // tiles
    entries = tiles * cap
    columns = views * PW * PH // slabs
    copies = slabs // views
    direct = cap % LANES == 0
    vmem = pl.BlockSpec(memory_space=pltpu.VMEM)

    out_shape = (slabs * tiles * NF, cap) if direct else (views, NF, entries)
    sent = pl.pallas_call(
        partial(sender_kernel, views, tiles, copies, direct),
        out_shape=pltpu.VMEM(out_shape, f32),
        in_specs=[vmem] * 7,
        out_specs=vmem,
        scratch_shapes=[pltpu.VMEM((views, 16, rows), f32)],
        name="sender",
    )(centers, scale, angle, opacity, color.transpose(1, 0, 2), rank, dest.transpose(0, 1, 3, 2))
    if not direct:
        sent = sent.reshape(views, 1, NF, tiles, cap).transpose(0, 1, 3, 2, 4)
        sent = jnp.broadcast_to(sent, (views, copies, tiles, NF, cap)).reshape(slabs * tiles, 1, NF * cap)
    sent = sent.reshape(slabs * tiles, 1, NF * cap)
    got = lax.all_to_all(sent, ("slab", "tile"), split_axis=0, concat_axis=0, tiled=True)
    if direct:
        got = got.reshape(slabs * tiles * NF, cap)
    else:
        got = got.reshape(slabs, tiles, NF, cap).transpose(2, 0, 1, 3).reshape(NF, slabs, entries)
    lanes = entries // STEPS * GROUP
    return pl.pallas_call(
        partial(receiver_kernel, slabs, tiles, views, direct, tiles * rows),
        out_shape=jax.ShapeDtypeStruct((4, 1, columns), f32),
        in_specs=[pl.BlockSpec(memory_space=pl.ANY), vmem],
        out_specs=vmem,
        scratch_shapes=[
            pltpu.VMEM((entries // LANES, GROUP * slabs, LANES), f32),
            pltpu.VMEM((lanes // LANES, STEPS * slabs, LANES), f32),
            pltpu.VMEM((2 * LANES - GROUP, columns), f32),
            pltpu.VMEM((6 * slabs, columns), f32),
            pltpu.VMEM((slabs // 8 * columns // LANES, 8, LANES), f32),
            pltpu.SMEM(order.shape, jnp.int32),
            pltpu.SemaphoreType.DMA,
        ],
        name="receiver",
    )(order, pltpu.with_memory_space_constraint(got, pltpu.VMEM))


def solution(mesh):
    in_specs = (
        P("slab", None, None, "tile"),
        P("slab", None, None, "tile"),
        P("slab", None, "tile"),
        P("slab", "tile"),
        P("slab", None, "tile"),
        P("slab", None, "tile"),
        P("slab", None, "tile", None),
        P(),
    )
    return jax.shard_map(
        partial(body, mesh.shape["slab"], mesh.shape["tile"]),
        mesh=mesh,
        in_specs=in_specs,
        out_specs=P(None, "tile", "slab"),
        check_vma=False,
    )
```

```python
from functools import partial
import math

import jax
import jax.numpy as jnp
from jax import lax
from jax.experimental import pallas as pl
from jax.experimental.pallas import tpu as pltpu
from jax.sharding import PartitionSpec as P

PW = 64
PH = 32
NF = 10
HALF_LOG2E = 0.5 * math.log2(math.e)
X_MID = 16.0
LANES = 128
GROUP = 32
PART = 16
AHEAD = 2
LAG = 2
STOPS = (5, 6, 7, 8, 9, 16)
STEPS = 128
VALID = 24
COLOR = 25

f32 = jnp.float32
bf16 = jnp.bfloat16
NT = (((1,), (1,)), ((), ()))


def pieces(x, count):
    out = []
    for _ in range(count):
        part = x.astype(bf16)
        out.append(part)
        x = x - part.astype(f32)
    return out


def mark(condition):
    return jnp.where(condition, jnp.ones(condition.shape, bf16), jnp.zeros(condition.shape, bf16))


def sender_kernel(views, tiles, copies, direct, centers, scale, angle, opacity, color, rank, dest, out, feat):
    rows = centers.shape[3]
    cap = 2 * rows // tiles
    slots = tiles * cap
    hot_rows = -(-tiles // 16) * 16

    theta = angle[0]
    cosine = jnp.cos(theta)
    sine = jnp.sin(theta)
    feat[...] = jnp.zeros_like(feat)
    def count_up(shape, axis):
        return lax.broadcasted_iota(jnp.int32, shape, axis).astype(f32).astype(bf16)

    before = mark(count_up((rows, rows), 0) < count_up((rows, rows), 1))
    tile_id = lax.broadcasted_iota(jnp.int32, (hot_rows, rows), 0)
    slot_id = count_up((cap, rows), 0)
    hot = [jnp.where(tile_id == dest[0, v], 1.0, 0.0) for v in range(views)]
    hot = jnp.concatenate(hot, axis=0)
    earlier = hot * jnp.dot(hot.astype(bf16), before, preferred_element_type=f32)
    for v in range(views):
        feat[v, 0:2] = centers[0, v]
        s1 = scale[0, v, 0:1]
        s2 = scale[0, v, 1:2]
        i1 = 1.0 / (s1 * s1)
        i2 = 1.0 / (s2 * s2)
        c = cosine[v : v + 1]
        s = sine[v : v + 1]
        feat[v, 2:3] = c * c * i1 + s * s * i2
        feat[v, 3:4] = c * s * (i1 - i2)
        feat[v, 4:5] = s * s * i1 + c * c * i2
        feat[v, 5:6] = opacity[0:1]
        for i in range(3):
            feat[v, 6 + i : 7 + i] = color[i]
        feat[v, 9:10] = rank[0, v : v + 1].astype(f32)
    for v in range(views):
        place = jnp.sum(earlier[v * hot_rows : (v + 1) * hot_rows], axis=0, keepdims=True)
        slot = dest[0, v].astype(f32) * cap + place
        pick = [mark(jnp.broadcast_to((slot - t * cap).astype(bf16), (cap, rows)) == slot_id) for t in range(tiles)]
        pick = jnp.concatenate(pick, axis=0)
        stack = jnp.concatenate(pieces(feat[v], 3), axis=0)
        moved = lax.dot_general(stack, pick, NT, preferred_element_type=f32)
        moved = moved[0:16] + moved[16:32] + moved[32:48]
        if direct:
            for t in range(tiles):
                block = moved[0:NF, t * cap : (t + 1) * cap]
                for q in range(copies):
                    out[pl.ds((t * views * copies + v * copies + q) * NF, NF), :] = block
        else:
            out[v] = moved[0:NF]


def positions(rank, real, slabs, n_ranks):
    entries = rank.shape[1]
    tall = 32
    wide = -(-n_ranks // tall)
    high = jnp.floor(rank * (1.0 / wide))
    low = (rank - high * wide).astype(bf16)
    high = jnp.where(real, high, 2.0 * tall)
    high_b = high.astype(bf16)
    tall_f = lax.broadcasted_iota(jnp.int32, (tall, entries), 0).astype(f32)
    tall_b = tall_f.astype(bf16)
    wide_b = lax.broadcasted_iota(jnp.int32, (wide, entries), 0).astype(f32).astype(bf16)
    ones = jnp.ones((wide, entries), bf16)

    fronts = []
    for k in range(slabs):
        hi = jnp.broadcast_to(high_b[k : k + 1], (tall, entries))
        lo = jnp.broadcast_to(low[k : k + 1], (wide, entries))
        left = jnp.concatenate([mark(hi == tall_b), mark(hi < tall_b)], axis=1)
        right = jnp.concatenate([mark(lo < wide_b), ones], axis=1)
        front = lax.dot_general(left, right, NT, preferred_element_type=f32)
        fronts.append(jnp.concatenate(pieces(front, 2), axis=1))
    out = []
    for k in range(slabs):
        is_lo = mark(jnp.broadcast_to(low[k : k + 1], (wide, entries)) == wide_b)
        mine = jnp.dot(fronts[k], jnp.concatenate([is_lo, is_lo], axis=0), preferred_element_type=f32)
        mine = jnp.where(high[k : k + 1] == tall_f, mine, 0.0)
        out.append(jnp.sum(mine, axis=0, keepdims=True))
    return jnp.where(real, jnp.concatenate(out, axis=0), -1.0)


def receiver_kernel(slabs, tiles, views, direct, n_ranks, order_hbm, recv, out, coef, lists, basis, acc, kept, order, order_sem):
    entries = coef.shape[0] * LANES
    columns = out.shape[2]
    blocks = columns // LANES
    pixels = PW * PH
    groups = slabs // 8
    chunks = entries // STEPS
    per_row = LANES // GROUP
    shades = 3 * slabs

    fetch = pltpu.make_async_copy(order_hbm, order, order_sem)
    fetch.start()
    me = lax.axis_index("slab")
    first = me * columns
    view = first // pixels
    y_first = (first - view * pixels) // PW
    half_rows = columns // PW // 2
    y_mid = (y_first + half_rows).astype(f32)

    def feature(f):
        if direct:
            return jnp.concatenate(
                [recv[pl.ds(t * slabs * NF + f, slabs, stride=NF), :] for t in range(tiles)], axis=1
            )
        return recv[f]

    o = feature(5)
    real = o > 0.0
    longest = jnp.max(jnp.sum(jnp.where(real, 1.0, 0.0), axis=1))
    place = positions(feature(9), real, slabs, n_ranks)
    x = feature(0) - X_MID
    y = feature(1) - y_mid
    a = feature(2)
    b = feature(3)
    c = feature(4)
    h = -HALF_LOG2E
    ax_by = a * x + b * y
    bx_cy = b * x + c * y
    constant = h * (x * ax_by + y * bx_cy) + jnp.log2(jnp.where(real, o, 1.0))
    table_rows = []
    for one, count in ((h * a, 2), ((2.0 * h) * b, 2), (h * c, 1)):
        table_rows += [p.astype(f32) for p in pieces(one, 3)] * count
    for one in ((-2.0 * h) * ax_by, (-2.0 * h) * bx_cy, constant):
        table_rows += [p.astype(f32) for p in pieces(one, 3)]
    table_rows.append(jnp.ones_like(o))
    colors = [[p.astype(f32) for p in pieces(feature(6 + i), 2)] for i in range(3)]
    table_rows += [p[0] for p in colors] + [p[1] for p in colors]
    table_rows += [jnp.zeros_like(o)] * (GROUP - len(table_rows))
    for i, one in enumerate(table_rows):
        for t in range(entries // LANES):
            coef[t, i * slabs : (i + 1) * slabs, :] = one[:, t * LANES : (t + 1) * LANES]

    lane = lax.broadcasted_iota(jnp.int32, (1, columns), 1)
    row = lane // PW
    u = (lane - row * PW).astype(f32) + (0.5 - X_MID)
    w = (row - half_rows).astype(f32) + 0.5
    basis_rows = []
    for one, count in ((u * u, 2), (u * w, 2), (w * w, 1)):
        for part in pieces(one, count):
            basis_rows += [part.astype(f32)] * 3
    basis_rows += [u] * 3 + [w] * 3 + [jnp.ones_like(u)] * 3 + [jnp.full_like(u, 400.0)]
    basis[...] = jnp.zeros_like(basis)
    for i, one in enumerate(basis_rows):
        basis[LANES - GROUP + i : LANES - GROUP + i + 1] = one

    missing = jnp.where(lax.broadcasted_iota(jnp.int32, (1, chunks * GROUP), 1) % GROUP == VALID, -1.0, 0.0)
    want = lax.broadcasted_iota(jnp.int32, (STEPS, entries), 0).astype(f32).astype(bf16)
    place_group = jnp.floor(place * (1.0 / STEPS))
    place_step = (place - place_group * STEPS).astype(bf16)
    place_group = place_group.astype(bf16)
    for k in range(slabs):
        table = [coef[t, pl.ds(k, GROUP, stride=slabs), :] for t in range(entries // LANES)]
        table = jnp.concatenate(table, axis=1).astype(bf16)
        group = jnp.broadcast_to(place_group[k : k + 1], (GROUP, entries))
        spread = [
            jnp.where(group == jnp.full((GROUP, entries), g, bf16), table, jnp.zeros_like(table)) for g in range(chunks)
        ]
        spread = jnp.concatenate(spread, axis=0)
        pick = mark(jnp.broadcast_to(place_step[k : k + 1], (STEPS, entries)) == want)
        got = lax.dot_general(pick, spread, NT, preferred_element_type=f32) + missing
        for t in range(chunks // per_row):
            lists[t, pl.ds(k, STEPS, stride=slabs), :] = got[:, t * LANES : (t + 1) * LANES]

    own = lax.broadcasted_iota(jnp.int32, (slabs, PART * slabs), 0)
    own = own == lax.broadcasted_iota(jnp.int32, (slabs, PART * slabs), 1) % slabs

    rows = PART * slabs
    per_chunk = STEPS // PART

    parts = chunks * per_chunk
    ones = jnp.ones((8, LANES), f32)

    def exponents(sorted_lists, n):
        g, p = n // per_chunk, n % per_chunk
        first_row = LANES - GROUP - g % per_row * GROUP
        monomials = basis[first_row : first_row + LANES].astype(bf16)
        lhs = sorted_lists[g // per_row][p * rows : (p + 1) * rows]
        return jnp.dot(lhs, monomials, preferred_element_type=f32)

    def weights(q, keep):
        highs = []
        lows = []
        for r in range(0, rows, 16):
            hi_row = []
            lo_row = []
            for l in range(blocks):
                both = []
                for at in (r, r + 8):
                    i = at // 8 % groups * blocks + l
                    one = jnp.exp2(q[at : at + 8, l * LANES : (l + 1) * LANES]) * keep[i]
                    keep[i] = keep[i] - one
                    both.append(one)
                hi, lo = pieces(jnp.concatenate(both, axis=0), 2)
                hi_row.append(hi)
                lo_row.append(lo)
            highs.append(jnp.concatenate(hi_row, axis=1))
            lows.append(jnp.concatenate(lo_row, axis=1))
        return jnp.concatenate(highs + lows, axis=0)

    def colours(shade_rows, n):
        g, p = n // per_chunk, n % per_chunk
        some = shade_rows[g // per_row][g % per_row * 8 : g % per_row * 8 + 8, p * rows : (p + 1) * rows]
        some = [jnp.where(own, some[i : i + 1], 0.0) for i in range(6)]
        some = jnp.concatenate(some, axis=0).astype(bf16)
        return jnp.concatenate([some, some], axis=1)

    def blend(parts):
        sorted_lists = [lists[t].astype(bf16) for t in range(chunks // per_row)]
        keep = [ones] * (groups * blocks)
        total = jnp.zeros((6 * slabs, columns), f32)
        ahead = [exponents(sorted_lists, n) for n in range(AHEAD)]
        shade_rows = []
        for t in range(chunks // per_row):
            r = lax.broadcasted_iota(jnp.int32, (per_row * 8, LANES), 0)
            choose = lax.broadcasted_iota(jnp.int32, (per_row * 8, LANES), 1) == r // 8 * GROUP + COLOR + r % 8
            choose = jnp.where(choose & (r % 8 < 6), 1.0, 0.0).astype(bf16)
            shade_rows.append(lax.dot_general(choose, sorted_lists[t], NT, preferred_element_type=f32))

        behind = []
        for n in range(parts + LAG):
            if n >= LAG:
                total = total + jnp.dot(colours(shade_rows, n - LAG), behind.pop(0), preferred_element_type=f32)
            if n + AHEAD < parts:
                ahead.append(exponents(sorted_lists, n + AHEAD))
            if n < parts:
                behind.append(weights(ahead.pop(0), keep))
        acc[...] = total
        for i, one in enumerate(keep):
            kept[i] = one

    floor = -1
    for sixteenths in STOPS:
        most = parts * sixteenths // 16
        fits = (longest > floor * PART) & (longest <= most * PART)
        pl.when(fits)(partial(blend, most))
        floor = most
    keep = [kept[i] for i in range(groups * blocks)]

    fetch.wait()
    sub = lax.broadcasted_iota(jnp.int32, (8, LANES), 0)
    orders = []
    for g in range(groups):
        mine = jnp.zeros((8, LANES), jnp.int32)
        for r in range(8):
            mine = jnp.where(sub == r, order[view, g * 8 + r], mine)
        orders.append(mine)
    for l in range(blocks):
        at = slice(l * LANES, (l + 1) * LANES)
        prefix = [ones] * groups
        total = jnp.ones((1, LANES), f32)
        for k in range(slabs):
            other = keep[k // 8 * blocks + l][k % 8 : k % 8 + 1]
            total = total * other
            rank_k = order[view, k]
            for g in range(groups):
                prefix[g] = prefix[g] * jnp.where(rank_k < orders[g], other, 1.0)
        for m in range(3):
            value = jnp.zeros((1, LANES), f32)
            for g in range(groups):
                r = m * slabs + g * 8
                value = value + jnp.sum(
                    prefix[g] * (acc[r : r + 8, at] + acc[shades + r : shades + r + 8, at]), axis=0, keepdims=True
                )
            out[m, :, at] = value
        out[3, :, at] = total


def body(slabs, tiles, centers, scale, angle, opacity, color, rank, dest, order):
    views = centers.shape[1]
    rows = centers.shape[3]
    cap = 2 * rows // tiles
    entries = tiles * cap
    columns = views * PW * PH // slabs
    copies = slabs // views
    direct = cap % LANES == 0
    vmem = pl.BlockSpec(memory_space=pltpu.VMEM)

    out_shape = (slabs * tiles * NF, cap) if direct else (views, NF, entries)
    sent = pl.pallas_call(
        partial(sender_kernel, views, tiles, copies, direct),
        out_shape=pltpu.VMEM(out_shape, f32),
        in_specs=[vmem] * 7,
        out_specs=vmem,
        scratch_shapes=[pltpu.VMEM((views, 16, rows), f32)],
        name="sender",
    )(centers, scale, angle, opacity, color.transpose(1, 0, 2), rank, dest.transpose(0, 1, 3, 2))
    if not direct:
        sent = sent.reshape(views, NF, tiles, cap).transpose(2, 0, 1, 3)
        sent = jnp.broadcast_to(sent[:, :, None], (tiles, views, copies, NF, cap))
    sent = sent.reshape(slabs * tiles, 1, NF * cap)
    got = lax.all_to_all(sent, ("tile", "slab"), split_axis=0, concat_axis=0, tiled=True)
    if direct:
        got = got.reshape(slabs * tiles * NF, cap)
    else:
        got = got.reshape(tiles, slabs, NF, cap).transpose(2, 1, 0, 3).reshape(NF, slabs, entries)
    lanes = entries // STEPS * GROUP
    return pl.pallas_call(
        partial(receiver_kernel, slabs, tiles, views, direct, tiles * rows),
        out_shape=jax.ShapeDtypeStruct((4, 1, columns), f32),
        in_specs=[pl.BlockSpec(memory_space=pl.ANY), vmem],
        out_specs=vmem,
        scratch_shapes=[
            pltpu.VMEM((entries // LANES, GROUP * slabs, LANES), f32),
            pltpu.VMEM((lanes // LANES, STEPS * slabs, LANES), f32),
            pltpu.VMEM((2 * LANES - GROUP, columns), f32),
            pltpu.VMEM((6 * slabs, columns), f32),
            pltpu.VMEM((slabs // 8 * columns // LANES, 8, LANES), f32),
            pltpu.SMEM(order.shape, jnp.int32),
            pltpu.SemaphoreType.DMA,
        ],
        name="receiver",
    )(order, pltpu.with_memory_space_constraint(got, pltpu.VMEM))


def solution(mesh):
    in_specs = (
        P("slab", None, None, "tile"),
        P("slab", None, None, "tile"),
        P("slab", None, "tile"),
        P("slab", "tile"),
        P("slab", None, "tile"),
        P("slab", None, "tile"),
        P("slab", None, "tile", None),
        P(),
    )
    return jax.shard_map(
        partial(body, mesh.shape["slab"], mesh.shape["tile"]),
        mesh=mesh,
        in_specs=in_specs,
        out_specs=P(None, "tile", "slab"),
        check_vma=False,
    )
```

```python
from functools import partial
import math

import jax
import jax.numpy as jnp
from jax import lax
from jax.experimental import pallas as pl
from jax.experimental.pallas import tpu as pltpu
from jax.sharding import PartitionSpec as P

PW = 64
PH = 32
NF = 10
HALF_LOG2E = 0.5 * math.log2(math.e)
X_MID = 16.0
LANES = 128
GROUP = 32
PART = 16
AHEAD = 2
LAG = 2
STOPS = (5, 6, 7, 8, 9, 10, 12, 16)
STEPS = 128
VALID = 24
COLOR = 25

f32 = jnp.float32
bf16 = jnp.bfloat16
NT = (((1,), (1,)), ((), ()))


def pieces(x, count):
    out = []
    for _ in range(count):
        part = x.astype(bf16)
        out.append(part)
        x = x - part.astype(f32)
    return out


def mark(condition):
    return jnp.where(condition, jnp.ones(condition.shape, bf16), jnp.zeros(condition.shape, bf16))


def sender_kernel(views, tiles, copies, direct, centers, scale, angle, opacity, color, rank, dest, out, feat):
    rows = centers.shape[3]
    cap = 2 * rows // tiles
    slots = tiles * cap
    hot_rows = -(-tiles // 16) * 16

    theta = angle[0]
    cosine = jnp.cos(theta)
    sine = jnp.sin(theta)
    feat[...] = jnp.zeros_like(feat)
    def count_up(shape, axis):
        return lax.broadcasted_iota(jnp.int32, shape, axis).astype(f32).astype(bf16)

    before = mark(count_up((rows, rows), 0) < count_up((rows, rows), 1))
    tile_id = lax.broadcasted_iota(jnp.int32, (hot_rows, rows), 0)
    slot_id = count_up((cap, rows), 0)
    hot = [jnp.where(tile_id == dest[0, v], 1.0, 0.0) for v in range(views)]
    hot = jnp.concatenate(hot, axis=0)
    earlier = hot * jnp.dot(hot.astype(bf16), before, preferred_element_type=f32)
    for v in range(views):
        feat[v, 0:2] = centers[0, v]
        s1 = scale[0, v, 0:1]
        s2 = scale[0, v, 1:2]
        i1 = 1.0 / (s1 * s1)
        i2 = 1.0 / (s2 * s2)
        c = cosine[v : v + 1]
        s = sine[v : v + 1]
        feat[v, 2:3] = c * c * i1 + s * s * i2
        feat[v, 3:4] = c * s * (i1 - i2)
        feat[v, 4:5] = s * s * i1 + c * c * i2
        feat[v, 5:6] = opacity[0:1]
        for i in range(3):
            feat[v, 6 + i : 7 + i] = color[i]
        feat[v, 9:10] = rank[0, v : v + 1].astype(f32)
    for v in range(views):
        place = jnp.sum(earlier[v * hot_rows : (v + 1) * hot_rows], axis=0, keepdims=True)
        slot = dest[0, v].astype(f32) * cap + place
        pick = [mark(jnp.broadcast_to((slot - t * cap).astype(bf16), (cap, rows)) == slot_id) for t in range(tiles)]
        pick = jnp.concatenate(pick, axis=0)
        stack = jnp.concatenate(pieces(feat[v], 3), axis=0)
        moved = lax.dot_general(stack, pick, NT, preferred_element_type=f32)
        moved = moved[0:16] + moved[16:32] + moved[32:48]
        if direct:
            for t in range(tiles):
                block = moved[0:NF, t * cap : (t + 1) * cap]
                for q in range(copies):
                    out[pl.ds((t * views * copies + v * copies + q) * NF, NF), :] = block
        else:
            out[v] = moved[0:NF]


def positions(rank, real, slabs, n_ranks):
    entries = rank.shape[1]
    tall = 32
    wide = -(-n_ranks // tall)
    high = jnp.floor(rank * (1.0 / wide))
    low = (rank - high * wide).astype(bf16)
    high = jnp.where(real, high, 2.0 * tall)
    high_b = high.astype(bf16)
    tall_f = lax.broadcasted_iota(jnp.int32, (tall, entries), 0).astype(f32)
    tall_b = tall_f.astype(bf16)
    wide_b = lax.broadcasted_iota(jnp.int32, (wide, entries), 0).astype(f32).astype(bf16)
    ones = jnp.ones((wide, entries), bf16)

    fronts = []
    for k in range(slabs):
        hi = jnp.broadcast_to(high_b[k : k + 1], (tall, entries))
        lo = jnp.broadcast_to(low[k : k + 1], (wide, entries))
        left = jnp.concatenate([mark(hi == tall_b), mark(hi < tall_b)], axis=1)
        right = jnp.concatenate([mark(lo < wide_b), ones], axis=1)
        front = lax.dot_general(left, right, NT, preferred_element_type=f32)
        fronts.append(jnp.concatenate(pieces(front, 2), axis=1))
    out = []
    for k in range(slabs):
        is_lo = mark(jnp.broadcast_to(low[k : k + 1], (wide, entries)) == wide_b)
        mine = jnp.dot(fronts[k], jnp.concatenate([is_lo, is_lo], axis=0), preferred_element_type=f32)
        mine = jnp.where(high[k : k + 1] == tall_f, mine, 0.0)
        out.append(jnp.sum(mine, axis=0, keepdims=True))
    return jnp.where(real, jnp.concatenate(out, axis=0), -1.0)


def receiver_kernel(slabs, tiles, views, direct, n_ranks, order_hbm, recv, out, coef, lists, basis, acc, kept, order, order_sem):
    entries = coef.shape[0] * LANES
    columns = out.shape[2]
    blocks = columns // LANES
    pixels = PW * PH
    groups = slabs // 8
    chunks = entries // STEPS
    per_row = LANES // GROUP
    shades = 3 * slabs

    fetch = pltpu.make_async_copy(order_hbm, order, order_sem)
    fetch.start()
    me = lax.axis_index("slab")
    first = me * columns
    view = first // pixels
    y_first = (first - view * pixels) // PW
    half_rows = columns // PW // 2
    y_mid = (y_first + half_rows).astype(f32)

    def feature(f):
        if direct:
            return jnp.concatenate(
                [recv[pl.ds(t * slabs * NF + f, slabs, stride=NF), :] for t in range(tiles)], axis=1
            )
        return recv[f]

    o = feature(5)
    real = o > 0.0
    longest = jnp.max(jnp.sum(jnp.where(real, 1.0, 0.0), axis=1))
    place = positions(feature(9), real, slabs, n_ranks)
    x = feature(0) - X_MID
    y = feature(1) - y_mid
    a = feature(2)
    b = feature(3)
    c = feature(4)
    h = -HALF_LOG2E
    ax_by = a * x + b * y
    bx_cy = b * x + c * y
    constant = h * (x * ax_by + y * bx_cy) + jnp.log2(jnp.where(real, o, 1.0))
    table_rows = []
    for one, count in ((h * a, 2), ((2.0 * h) * b, 2), (h * c, 1)):
        table_rows += [p.astype(f32) for p in pieces(one, 3)] * count
    for one in ((-2.0 * h) * ax_by, (-2.0 * h) * bx_cy, constant):
        table_rows += [p.astype(f32) for p in pieces(one, 3)]
    table_rows.append(jnp.ones_like(o))
    colors = [[p.astype(f32) for p in pieces(feature(6 + i), 2)] for i in range(3)]
    table_rows += [p[0] for p in colors] + [p[1] for p in colors]
    table_rows += [jnp.zeros_like(o)] * (GROUP - len(table_rows))
    for i, one in enumerate(table_rows):
        for t in range(entries // LANES):
            coef[t, i * slabs : (i + 1) * slabs, :] = one[:, t * LANES : (t + 1) * LANES]

    lane = lax.broadcasted_iota(jnp.int32, (1, columns), 1)
    row = lane // PW
    u = (lane - row * PW).astype(f32) + (0.5 - X_MID)
    w = (row - half_rows).astype(f32) + 0.5
    basis_rows = []
    for one, count in ((u * u, 2), (u * w, 2), (w * w, 1)):
        for part in pieces(one, count):
            basis_rows += [part.astype(f32)] * 3
    basis_rows += [u] * 3 + [w] * 3 + [jnp.ones_like(u)] * 3 + [jnp.full_like(u, 400.0)]
    basis[...] = jnp.zeros_like(basis)
    for i, one in enumerate(basis_rows):
        basis[LANES - GROUP + i : LANES - GROUP + i + 1] = one

    missing = jnp.where(lax.broadcasted_iota(jnp.int32, (1, chunks * GROUP), 1) % GROUP == VALID, -1.0, 0.0)
    want = lax.broadcasted_iota(jnp.int32, (STEPS, entries), 0).astype(f32).astype(bf16)
    place_group = jnp.floor(place * (1.0 / STEPS))
    place_step = (place - place_group * STEPS).astype(bf16)
    place_group = place_group.astype(bf16)
    for k in range(slabs):
        table = [coef[t, pl.ds(k, GROUP, stride=slabs), :] for t in range(entries // LANES)]
        table = jnp.concatenate(table, axis=1).astype(bf16)
        group = jnp.broadcast_to(place_group[k : k + 1], (GROUP, entries))
        spread = [
            jnp.where(group == jnp.full((GROUP, entries), g, bf16), table, jnp.zeros_like(table)) for g in range(chunks)
        ]
        spread = jnp.concatenate(spread, axis=0)
        pick = mark(jnp.broadcast_to(place_step[k : k + 1], (STEPS, entries)) == want)
        got = lax.dot_general(pick, spread, NT, preferred_element_type=f32) + missing
        for t in range(chunks // per_row):
            lists[t, pl.ds(k, STEPS, stride=slabs), :] = got[:, t * LANES : (t + 1) * LANES]

    own = lax.broadcasted_iota(jnp.int32, (slabs, PART * slabs), 0)
    own = own == lax.broadcasted_iota(jnp.int32, (slabs, PART * slabs), 1) % slabs

    rows = PART * slabs
    per_chunk = STEPS // PART

    parts = chunks * per_chunk
    ones = jnp.ones((8, LANES), f32)

    def exponents(sorted_lists, n):
        g, p = n // per_chunk, n % per_chunk
        first_row = LANES - GROUP - g % per_row * GROUP
        monomials = basis[first_row : first_row + LANES].astype(bf16)
        lhs = sorted_lists[g // per_row][p * rows : (p + 1) * rows]
        return jnp.dot(lhs, monomials, preferred_element_type=f32)

    def weights(q, keep):
        highs = []
        lows = []
        for r in range(0, rows, 16):
            hi_row = []
            lo_row = []
            for l in range(blocks):
                both = []
                for at in (r, r + 8):
                    i = at // 8 % groups * blocks + l
                    one = jnp.exp2(q[at : at + 8, l * LANES : (l + 1) * LANES]) * keep[i]
                    keep[i] = keep[i] - one
                    both.append(one)
                hi, lo = pieces(jnp.concatenate(both, axis=0), 2)
                hi_row.append(hi)
                lo_row.append(lo)
            highs.append(jnp.concatenate(hi_row, axis=1))
            lows.append(jnp.concatenate(lo_row, axis=1))
        return jnp.concatenate(highs + lows, axis=0)

    def colours(shade_rows, n):
        g, p = n // per_chunk, n % per_chunk
        some = shade_rows[g // per_row][g % per_row * 8 : g % per_row * 8 + 8, p * rows : (p + 1) * rows]
        some = [jnp.where(own, some[i : i + 1], 0.0) for i in range(6)]
        some = jnp.concatenate(some, axis=0).astype(bf16)
        return jnp.concatenate([some, some], axis=1)

    def blend(parts):
        sorted_lists = [lists[t].astype(bf16) for t in range(chunks // per_row)]
        keep = [ones] * (groups * blocks)
        total = jnp.zeros((6 * slabs, columns), f32)
        ahead = [exponents(sorted_lists, n) for n in range(AHEAD)]
        shade_rows = []
        for t in range(chunks // per_row):
            r = lax.broadcasted_iota(jnp.int32, (per_row * 8, LANES), 0)
            choose = lax.broadcasted_iota(jnp.int32, (per_row * 8, LANES), 1) == r // 8 * GROUP + COLOR + r % 8
            choose = jnp.where(choose & (r % 8 < 6), 1.0, 0.0).astype(bf16)
            shade_rows.append(lax.dot_general(choose, sorted_lists[t], NT, preferred_element_type=f32))

        behind = []
        for n in range(parts + LAG):
            if n >= LAG:
                total = total + jnp.dot(colours(shade_rows, n - LAG), behind.pop(0), preferred_element_type=f32)
            if n + AHEAD < parts:
                ahead.append(exponents(sorted_lists, n + AHEAD))
            if n < parts:
                behind.append(weights(ahead.pop(0), keep))
        acc[...] = total
        for i, one in enumerate(keep):
            kept[i] = one

    floor = -1
    for sixteenths in STOPS:
        most = parts * sixteenths // 16
        fits = (longest > floor * PART) & (longest <= most * PART)
        pl.when(fits)(partial(blend, most))
        floor = most
    keep = [kept[i] for i in range(groups * blocks)]

    fetch.wait()
    sub = lax.broadcasted_iota(jnp.int32, (8, LANES), 0)
    orders = []
    for g in range(groups):
        mine = jnp.zeros((8, LANES), jnp.int32)
        for r in range(8):
            mine = jnp.where(sub == r, order[view, g * 8 + r], mine)
        orders.append(mine)
    for l in range(blocks):
        at = slice(l * LANES, (l + 1) * LANES)
        prefix = [ones] * groups
        total = jnp.ones((1, LANES), f32)
        for k in range(slabs):
            other = keep[k // 8 * blocks + l][k % 8 : k % 8 + 1]
            total = total * other
            rank_k = order[view, k]
            for g in range(groups):
                prefix[g] = prefix[g] * jnp.where(rank_k < orders[g], other, 1.0)
        for m in range(3):
            value = jnp.zeros((1, LANES), f32)
            for g in range(groups):
                r = m * slabs + g * 8
                value = value + jnp.sum(
                    prefix[g] * (acc[r : r + 8, at] + acc[shades + r : shades + r + 8, at]), axis=0, keepdims=True
                )
            out[m, :, at] = value
        out[3, :, at] = total


def body(slabs, tiles, centers, scale, angle, opacity, color, rank, dest, order):
    views = centers.shape[1]
    rows = centers.shape[3]
    cap = 2 * rows // tiles
    entries = tiles * cap
    columns = views * PW * PH // slabs
    copies = slabs // views
    direct = cap % LANES == 0
    vmem = pl.BlockSpec(memory_space=pltpu.VMEM)

    out_shape = (slabs * tiles * NF, cap) if direct else (views, NF, entries)
    sent = pl.pallas_call(
        partial(sender_kernel, views, tiles, copies, direct),
        out_shape=pltpu.VMEM(out_shape, f32),
        in_specs=[vmem] * 7,
        out_specs=vmem,
        scratch_shapes=[pltpu.VMEM((views, 16, rows), f32)],
        name="sender",
    )(centers, scale, angle, opacity, color.transpose(1, 0, 2), rank, dest.transpose(0, 1, 3, 2))
    if not direct:
        sent = sent.reshape(views, NF, tiles, cap).transpose(2, 0, 1, 3)
        sent = jnp.broadcast_to(sent[:, :, None], (tiles, views, copies, NF, cap))
    sent = sent.reshape(slabs * tiles, 1, NF * cap)
    got = lax.all_to_all(sent, ("tile", "slab"), split_axis=0, concat_axis=0, tiled=True)
    if direct:
        got = got.reshape(slabs * tiles * NF, cap)
    else:
        got = got.reshape(tiles, slabs, NF, cap).transpose(2, 1, 0, 3).reshape(NF, slabs, entries)
    lanes = entries // STEPS * GROUP
    return pl.pallas_call(
        partial(receiver_kernel, slabs, tiles, views, direct, tiles * rows),
        out_shape=jax.ShapeDtypeStruct((4, 1, columns), f32),
        in_specs=[pl.BlockSpec(memory_space=pl.ANY), vmem],
        out_specs=vmem,
        scratch_shapes=[
            pltpu.VMEM((entries // LANES, GROUP * slabs, LANES), f32),
            pltpu.VMEM((lanes // LANES, STEPS * slabs, LANES), f32),
            pltpu.VMEM((2 * LANES - GROUP, columns), f32),
            pltpu.VMEM((6 * slabs, columns), f32),
            pltpu.VMEM((slabs // 8 * columns // LANES, 8, LANES), f32),
            pltpu.SMEM(order.shape, jnp.int32),
            pltpu.SemaphoreType.DMA,
        ],
        name="receiver",
    )(order, pltpu.with_memory_space_constraint(got, pltpu.VMEM))


def solution(mesh):
    in_specs = (
        P("slab", None, None, "tile"),
        P("slab", None, None, "tile"),
        P("slab", None, "tile"),
        P("slab", "tile"),
        P("slab", None, "tile"),
        P("slab", None, "tile"),
        P("slab", None, "tile", None),
        P(),
    )
    return jax.shard_map(
        partial(body, mesh.shape["slab"], mesh.shape["tile"]),
        mesh=mesh,
        in_specs=in_specs,
        out_specs=P(None, "tile", "slab"),
        check_vma=False,
    )
```
